32 devices in a mesh: parts: 2 (over y), tm: 8 (over z, x), band: 2 (over core).
Axes of the slice: x: 2, y: 2, z: 4, core: 2. Of those that a mesh axis runs over, the one named last changes fastest.
Arguments:
- query_tokens: bfloat16 [16, 8, 32, 2240], P(('parts', 'tm'), 'band'), parts along dimension 0, may hold values from -6 to 6
- key_tokens: bfloat16 [16, 8, 32, 2240], P(('parts', 'tm'), 'band'), parts along dimension 0, may hold values from -6 to 6
- value_tokens: bfloat16 [16, 8, 32, 2240], P(('parts', 'tm'), 'band'), parts along dimension 0, may hold values from -14 to 14
- norm_gain: float32 [2240], replicated, may hold values from 0.1 to 1.9
- out_weight: bfloat16 [2, 8, 313600], P('band', 'tm'), may hold values from -0.125 to 0.125
Outputs:
- block_out: bfloat16 [16, 8, 32, 2240], P(('parts', 'tm'), 'band'), parts along dimension 0
The draws below stay inside these ranges and needn't reach their ends.
There are 2 independent parts, one for each index of `parts`. The reference program is written for one: setup_inputs(seed, part) draws one part's arguments, and reference() takes and returns one part's arrays. A program takes and returns all parts, laid end to end along the dimension named above; an argument that names none is the same for every part. Nothing has to cross between parts.
All inputs are finite; a program needn't handle non-finite values.
Results may differ from the reference program's by a relative error of at most 0.0049.
Values may be sent and summed in bfloat16 or wider, within the bound.
No kernel may reach another device: no remote copies, remote signals or barrier semaphores. Data moves between devices by JAX's collectives and lax.ppermute only.
A program may use at most 128 MiB of HBM per device.

```python
import math
import jax
import jax.numpy as jnp
from jax import lax

HEADS = 70
HD = 32
D = 2240
COLS = 32
FRAMES = 8
HEIGHT = 8
GROUP = 313600
N_TM = 8
N_BAND = 2


def draw_value_tokens(key, part):
    first, second = jax.random.split(jax.random.fold_in(key, 17), 2)
    channel_scale = jnp.exp(jax.random.uniform(first, (D,), jnp.float32, 0.0, math.log(10.0)))
    noise = jax.random.normal(second, (FRAMES, HEIGHT, COLS, D), jnp.float32)
    noise = jnp.clip(noise, -4.0, 4.0)
    return (noise * channel_scale / 3.0).astype(jnp.bfloat16)


def level_of(stream_key, extent, cuts, least, top_value):
    gain, own = 1.0, jax.random.fold_in(stream_key, 6)
    for dim, blocks in cuts:
        steps = jnp.exp(jax.random.uniform(jax.random.fold_in(own, dim), (blocks,), jnp.float32, least / len(cuts), top_value / len(cuts)))
        gain = gain * jnp.repeat(steps, extent[dim] // blocks).reshape([-1 if axis == dim else 1 for axis in range(len(extent))])
    return gain


def scatter_about(key, extent, scale, most, cuts=(), held_as=jnp.bfloat16):
    entries = scale * jax.random.normal(key, extent, jnp.float32)
    if cuts:
        entries = entries * level_of(key, extent, cuts, -0.22, 0.18)
    return jnp.clip(entries, -most, most).astype(held_as)


def setup_inputs(seed: int = 0, part: int = 0) -> dict:
    seeds = jax.random.split(jax.random.key(seed), 6)
    part_splits = jax.random.split(jax.random.fold_in(seeds[5], part), 6)
    query_tokens = scatter_about(part_splits[0], (FRAMES, HEIGHT, COLS, D), 1.0, 6.0, ((0, 8), (1, 2)))
    key_tokens = scatter_about(part_splits[1], (FRAMES, HEIGHT, COLS, D), 1.0, 6.0, ((0, 8), (1, 2)))
    value_tokens = draw_value_tokens(jax.random.fold_in(jax.random.fold_in(seeds[5], part), 71), part)
    norm_gain = jnp.clip(1.0 + 0.18 * jax.random.normal(seeds[3], (D,), jnp.float32), 0.1, 1.9)
    out_weight = scatter_about(seeds[4], (N_BAND, N_TM, GROUP), D ** -0.5, 0.125, ((0, 2), (1, 8)))
    return {"query_tokens": query_tokens, "key_tokens": key_tokens, "value_tokens": value_tokens, "norm_gain": norm_gain, "out_weight": out_weight}


norm_epsilon = 1e-06
read_epsilon = 1e-06

def frame_state(pieces):
    key_frame, value_frame = pieces
    key_relu = jax.nn.relu(key_frame.astype(jnp.float32)).reshape(-1, HEADS, HD)
    value_heads = value_frame.astype(jnp.float32).reshape(-1, HEADS, HD)
    state = jnp.einsum('thd,the->hde', key_relu, value_heads, precision=lax.Precision.HIGHEST)
    return (state, lax.optimization_barrier(jnp.sum(key_relu, axis=0)))

def frame_out(pieces, norm_gain, projection):
    query_frame, prefix_state, prefix_norm = pieces
    query_relu = jax.nn.relu(query_frame.astype(jnp.float32)).reshape(-1, HEADS, HD)
    numer = jnp.einsum('thd,hde->the', query_relu, prefix_state, precision=lax.Precision.HIGHEST)
    denom = jnp.einsum('thd,hd->th', query_relu, prefix_norm, precision=lax.Precision.HIGHEST) + read_epsilon
    reads = (numer / denom[:, :, None]).reshape(-1, D)
    square = lax.optimization_barrier(jnp.mean(reads * reads, axis=-1, keepdims=True))
    normed = (reads * lax.rsqrt(square + norm_epsilon) * norm_gain).astype(jnp.bfloat16)
    result = jnp.dot(normed, projection, preferred_element_type=jnp.float32)
    return result.astype(jnp.bfloat16).reshape(query_frame.shape)

def reference(query_tokens, key_tokens, value_tokens, norm_gain, out_weight):
    projection = out_weight.reshape(D, D)
    states, norms = lax.map(frame_state, (key_tokens, value_tokens))
    prefix_state = jnp.cumsum(states, axis=0)
    prefix_norm = jnp.cumsum(norms, axis=0)
    return lax.map(lambda pieces: frame_out(pieces, norm_gain, projection), (query_tokens, prefix_state, prefix_norm))
```

```python
import functools

import jax
import jax.numpy as jnp
from jax import lax
from jax.experimental import pallas as pl
from jax.experimental.pallas import tpu as pltpu
from jax.sharding import PartitionSpec as P

HEADS = 70
HD = 32
LANES = 128

norm_epsilon = 1e-06
read_epsilon = 1e-06

VMEM_LIMIT = 56 * 1024 * 1024


def round_up(n, m):
    return -(-n // m) * m


def call(kernel, out, args, scratch=(), flops=0, smem=0, name=None):
    whole = pl.BlockSpec(memory_space=pltpu.VMEM)
    scalar = pl.BlockSpec(memory_space=pltpu.SMEM)
    moved = sum(a.size * a.dtype.itemsize for a in jax.tree.leaves((args, out)))
    return pl.pallas_call(
        kernel,
        out_shape=out,
        in_specs=[scalar] * smem + [whole] * (len(args) - smem),
        out_specs=jax.tree.map(lambda _: whole, out),
        scratch_shapes=list(scratch),
        compiler_params=pltpu.CompilerParams(vmem_limit_bytes=VMEM_LIMIT),
        cost_estimate=pl.CostEstimate(flops=flops, bytes_accessed=moved, transcendentals=0),
        name=name,
    )(*args)


def shape(dims, dtype):
    return jax.ShapeDtypeStruct(tuple(dims), dtype)


def unpack_weight(rows, depth, at_ref, w_ref, mine_ref, rest_ref, tall):
    half = mine_ref.shape[1]
    tall[pl.ds(rows // 8 * 8, tall.shape[0] - rows // 8 * 8), :] = jnp.zeros(
        (tall.shape[0] - rows // 8 * 8, tall.shape[1]), jnp.float32
    )
    edge = depth // LANES * LANES
    tall[:, pl.ds(edge, tall.shape[1] - edge)] = jnp.zeros(
        (tall.shape[0], tall.shape[1] - edge), jnp.float32
    )
    for r in range(rows):
        tall[r : r + 1, 0:depth] = w_ref[0, :, depth * r : depth * (r + 1)].astype(jnp.float32)
    y = at_ref[0]
    mine_ref[...] = tall[:, pl.ds(pl.multiple_of(y * half, LANES), half)].astype(jnp.bfloat16)
    rest_ref[...] = tall[:, pl.ds(pl.multiple_of((1 - y) * half, LANES), half)].astype(jnp.bfloat16)


def head_mask():
    row = lax.broadcasted_iota(jnp.int32, (LANES, LANES), 0) // HD
    lane = lax.broadcasted_iota(jnp.int32, (LANES, LANES), 1) // HD
    return row == lane


def state_sums(half, at_ref, k_ref, v_ref, own_ref, other_ref, sums):
    depth = k_ref.shape[1]
    mask = head_mask()
    sums[...] = jnp.zeros_like(sums)
    for start in range(0, depth, LANES):
        n = min(LANES, depth - start)
        keys = jnp.maximum(k_ref[:, start : start + n], 0)
        values = v_ref[:, start : start + n]
        outer = lax.dot_general(
            values, keys, (((0,), (0,)), ((), ())), preferred_element_type=jnp.float32
        )
        outer = jnp.where(mask[:n, :n], outer, 0.0)
        folded = sum(outer[i : i + HD] for i in range(0, n, HD))
        sums[0:HD, start : start + n] = folded
        sums[HD : HD + 1, start : start + n] = jnp.sum(
            keys.astype(jnp.float32), axis=0, keepdims=True
        )
    own_ref[...] = jnp.zeros_like(own_ref)
    other_ref[...] = jnp.zeros_like(other_ref)

    @pl.when(at_ref[1] == 0)
    def _():
        own_ref[:, 0:half] = sums[:, 0:half]
        other_ref[:, 0:half] = sums[:, half : 2 * half]

    @pl.when(at_ref[1] != 0)
    def _():
        own_ref[:, 0:half] = sums[:, half : 2 * half]
        other_ref[:, 0:half] = sums[:, 0:half]


def read_states(half, shard, slots, at_ref, q_ref, p_ref, s_ref, g_ref, left_ref, square_ref, qh, gh, flat, blocks):
    count = q_ref.shape[0]
    qh[...] = jnp.zeros_like(qh)
    gh[...] = jnp.zeros_like(gh)

    def take(first):
        qh[0:count, 0:half] = q_ref[:, first : first + half]
        qh[count : 2 * count, 0:half] = p_ref[:, first : first + half]
        gh[:, 0:half] = g_ref[:, first : first + half]

    @pl.when(at_ref[1] == 0)
    def _():
        take(0)

    @pl.when(at_ref[1] != 0)
    def _():
        take(half)

    mask = head_mask()
    square = jnp.zeros((2 * count, LANES), jnp.float32)
    for start in range(0, qh.shape[1], LANES):
        query = jnp.maximum(qh[:, start : start + LANES], 0)
        state = s_ref[0:HD, start : start + LANES]
        total = s_ref[HD : HD + 1, start : start + LANES]
        spread = jnp.concatenate(
            [
                jnp.where(mask, jnp.concatenate([state] * (LANES // HD), axis=0), 0.0),
                jnp.where(mask, jnp.broadcast_to(total, (LANES, LANES)), 0.0),
            ],
            axis=0,
        )
        high = spread.astype(jnp.bfloat16)
        low = (spread - high.astype(jnp.float32)).astype(jnp.bfloat16)
        both = lax.dot_general(
            jnp.concatenate([query, query], axis=1),
            jnp.concatenate([high, low], axis=1),
            (((1,), (1,)), ((), ())),
            preferred_element_type=jnp.float32,
        )
        reads = both[:, 0:LANES] / (both[:, LANES : 2 * LANES] + read_epsilon)
        square += reads * reads
        flat[:, start : start + LANES] = (reads * gh[:, start : start + LANES]).astype(jnp.bfloat16)
    square_ref[...] = jnp.broadcast_to(
        jnp.sum(square, axis=1, keepdims=True), square_ref.shape
    )
    wide = left_ref.shape[1] // slots
    blocks[...] = jnp.zeros_like(blocks)
    for t in range(slots):
        blocks[t, :, 0:shard] = flat[:, shard * t : shard * (t + 1)]
    me = at_ref[2]
    for m in range(slots):
        left_ref[:, wide * m : wide * (m + 1)] = blocks[me ^ m]


def project(slots, spare, at_ref, left_ref, square_ref, *refs):
    mine, rest, (own_ref, other_ref) = refs[:slots], refs[slots : 2 * slots], refs[2 * slots :]
    count = left_ref.shape[0] // 2
    for i, pieces in enumerate((mine, rest)):
        weight = jnp.concatenate([p[...] for p in pieces], axis=0)
        total = jnp.dot(left_ref[...], weight, preferred_element_type=jnp.float32)
        own_ref[i] = total[:count]
        other_ref[i] = total[count:]
    last = 1 - at_ref[0]
    lane = lax.broadcasted_iota(jnp.int32, (count, LANES), 1)
    cut = spare // LANES * LANES
    for ref, first in ((own_ref, 0), (other_ref, count)):
        tail = ref[last, :, cut : cut + LANES]
        ref[last, :, cut : cut + LANES] = jnp.where(
            lane == spare % LANES, square_ref[first : first + count], tail
        )


def finish(depth, spare, at_ref, own_ref, got_ref, out_ref):
    half = own_ref.shape[2]
    first, last = at_ref[0], 1 - at_ref[0]
    right = own_ref[last] + got_ref[last]
    scale = lax.rsqrt(right[:, spare : spare + 1] / depth + norm_epsilon)
    out_ref[:, half:depth] = (right[:, : depth - half] * scale).astype(jnp.bfloat16)
    out_ref[:, 0:half] = ((own_ref[first] + got_ref[first]) * scale).astype(jnp.bfloat16)


def fast(query_tokens, key_tokens, value_tokens, norm_gain, out_weight):
    frames, rows, width, depth = query_tokens.shape
    count = rows * width
    bands, peers = lax.axis_size("band"), lax.axis_size("tm")
    half = depth // bands
    wide = round_up(half, LANES)
    shard = out_weight.shape[-1] // depth
    tall = round_up(shard, 16)
    cols = round_up(depth, 2 * LANES) // 2
    spare = depth - cols
    swap = [(0, 1), (1, 0)]

    def flip(x, mask):
        return lax.ppermute(x, "tm", [(i, i ^ mask) for i in range(peers)])

    def across(x, axis):
        return lax.ppermute(x, axis, swap)

    at = jnp.stack(
        [lax.axis_index("parts"), lax.axis_index("band"), lax.axis_index("tm")]
    ).astype(jnp.int32)
    bf16, f32 = jnp.bfloat16, jnp.float32

    mine, rest = {}, {}
    mine[0], rest[0] = call(
        functools.partial(unpack_weight, shard, depth),
        (shape((tall, cols), bf16), shape((tall, cols), bf16)),
        (at, out_weight),
        scratch=[pltpu.VMEM((tall, 2 * cols), f32)],
        smem=1,
        name="unpack_weight",
    )
    far = range(2, peers, 2)
    for m in far:
        mine[m] = flip(mine[0], m)
    mine[1], rest[1] = flip(mine[0], 1), flip(rest[0], 1)
    for m in far:
        mine[m + 1] = flip(mine[m], 1)
        rest[m] = across(mine[m], "parts")
    for m in far:
        rest[m + 1] = flip(rest[m], 1) if m == 2 else across(mine[m + 1], "parts")

    queries = query_tokens.reshape(count, depth)
    partner = across(queries, "band")
    own, other = call(
        functools.partial(state_sums, half),
        (shape((HD + 8, wide), f32), shape((HD + 8, wide), f32)),
        (at, key_tokens.reshape(count, depth), value_tokens.reshape(count, depth)),
        scratch=[pltpu.VMEM((HD + 8, round_up(depth, LANES)), f32)],
        smem=1,
        flops=2 * count * LANES * depth,
        name="state_sums",
    )
    total = own + across(other, "band")
    prefix = total
    bit = 1
    while bit < peers:
        got = flip(total, bit)
        prefix = prefix + jnp.where((at[2] & bit) != 0, got, 0.0)
        total = total + got
        bit *= 2
    left, square = call(
        functools.partial(read_states, half, shard, peers),
        (shape((2 * count, peers * tall), bf16), shape((2 * count, LANES), f32)),
        (at, queries, partner, prefix, norm_gain.reshape(1, depth)),
        scratch=[
            pltpu.VMEM((2 * count, wide), bf16),
            pltpu.VMEM((1, wide), f32),
            pltpu.VMEM((2 * count, wide), bf16),
            pltpu.VMEM((peers, 2 * count, tall), bf16),
        ],
        smem=1,
        flops=8 * count * LANES * wide,
        name="read_states",
    )

    own, other = call(
        functools.partial(project, peers, spare),
        (shape((2, count, cols), f32), shape((2, count, cols), f32)),
        (at, left, square, *[mine[m] for m in range(peers)], *[rest[m] for m in range(peers)]),
        smem=1,
        flops=8 * count * cols * peers * tall,
        name="project",
    )
    out = call(
        functools.partial(finish, depth, spare),
        shape((count, depth), bf16),
        (at, own, across(other, "band")),
        smem=1,
        name="finish",
    )
    return out.reshape(frames, rows, width, depth)


def entering(x, axis, combine, identity):
    peers, place = (lax.axis_size(axis), lax.axis_index(axis))
    everything = jax.tree.map(lambda part: lax.all_gather(part, axis), x)
    start = jax.tree.map(
        lambda part, zero: jnp.broadcast_to(jnp.asarray(zero, part.dtype), part.shape), x, identity
    )

    def hop(k, before):
        reached = k < place
        new = combine(before, jax.tree.map(lambda part: part[k], everything))
        return jax.tree.map(lambda a, b: jnp.where(reached, a, b), new, before)

    return lax.fori_loop(0, peers, hop, start)


def add_pair(earlier, later):
    return (earlier[0] + later[0], earlier[1] + later[1])


def general(query_tokens, key_tokens, value_tokens, norm_gain, out_weight):
    frames, rows, width, depth = query_tokens.shape
    key_relu = jax.nn.relu(key_tokens).reshape(frames, rows * width, HEADS, HD)
    value_heads = value_tokens.reshape(frames, rows * width, HEADS, HD)
    part_state = jnp.einsum(
        "fthd,fthe->fhde", key_relu, value_heads, preferred_element_type=jnp.float32
    ).reshape(frames, HEADS, HD * HD)
    part_norm = jnp.sum(key_relu, axis=1, dtype=jnp.float32)
    state_sum, norm_sum = lax.psum((part_state, part_norm), "band")
    local_state = jnp.cumsum(state_sum, axis=0)
    local_norm = jnp.cumsum(norm_sum, axis=0)
    before = entering(
        (local_state[-1], local_norm[-1]),
        "tm",
        add_pair,
        (jnp.zeros_like(local_state[-1]), jnp.zeros_like(local_norm[-1])),
    )
    prefix_state = local_state + before[0]
    prefix_norm = local_norm + before[1]
    query_relu = jax.nn.relu(query_tokens.astype(jnp.float32)).reshape(
        frames, rows * width, HEADS, HD
    )
    numer = jnp.einsum(
        "fthd,fhde->fthe",
        query_relu,
        prefix_state.reshape(frames, HEADS, HD, HD),
        precision=lax.Precision.HIGHEST,
    )
    denom = (
        jnp.einsum("fthd,fhd->fth", query_relu, prefix_norm, precision=lax.Precision.HIGHEST)
        + read_epsilon
    )
    reads = (numer / denom[:, :, :, None]).reshape(frames * rows * width, depth)
    square = jnp.mean(reads * reads, axis=-1, keepdims=True)
    normed = (reads * lax.rsqrt(square + norm_epsilon) * norm_gain).astype(jnp.bfloat16)
    gathered = lax.all_gather(out_weight, "tm", axis=1, tiled=True)
    rows_half = gathered.reshape(-1, depth)
    result = jnp.dot(
        normed,
        lax.all_gather(rows_half, "band", axis=0, tiled=True),
        preferred_element_type=jnp.float32,
    )
    return result.astype(jnp.bfloat16).reshape(frames, rows, width, depth)


def body(query_tokens, key_tokens, value_tokens, norm_gain, out_weight):
    frames, depth = query_tokens.shape[0], query_tokens.shape[-1]
    peers = lax.axis_size("tm")
    whole_rows = (
        frames == 1
        and lax.axis_size("band") == 2
        and lax.axis_size("parts") == 2
        and peers > 1
        and peers & (peers - 1) == 0
        and out_weight.shape[-1] % depth == 0
        and depth % (2 * HD) == 0
        and round_up(depth, 2 * LANES) > depth
    )
    run = fast if whole_rows else general
    return run(query_tokens, key_tokens, value_tokens, norm_gain, out_weight)


def solution(mesh):
    in_specs = (
        P(("parts", "tm"), "band", None, None),
        P(("parts", "tm"), "band", None, None),
        P(("parts", "tm"), "band", None, None),
        P(),
        P("band", "tm", None),
    )
    out_specs = P(("parts", "tm"), "band", None, None)
    return jax.shard_map(body, mesh=mesh, in_specs=in_specs, out_specs=out_specs, check_vma=False)
```

```python
import functools

import jax
import jax.numpy as jnp
from jax import lax
from jax.experimental import pallas as pl
from jax.experimental.pallas import tpu as pltpu
from jax.sharding import PartitionSpec as P


HEADS = 70
HD = 32
LANES = 128

norm_epsilon = 1e-06
read_epsilon = 1e-06


def round_up(n, m):
    return -(-n // m) * m


def call(kernel, out, args, scratch=(), flops=0, smem=0, mib=16):
    whole = pl.BlockSpec(memory_space=pltpu.VMEM)
    scalar = pl.BlockSpec(memory_space=pltpu.SMEM)
    moved = sum(a.size * a.dtype.itemsize for a in jax.tree.leaves((args, out)))
    return pl.pallas_call(
        kernel,
        out_shape=out,
        in_specs=[scalar] * smem + [whole] * (len(args) - smem),
        out_specs=jax.tree.map(lambda _: whole, out),
        scratch_shapes=list(scratch),
        compiler_params=pltpu.CompilerParams(vmem_limit_bytes=mib * 1024 * 1024),
        cost_estimate=pl.CostEstimate(flops=flops, bytes_accessed=moved, transcendentals=0),
    )(*args)


def shape(dims, dtype):
    return jax.ShapeDtypeStruct(tuple(dims), dtype)


def unpack_weight(rows, depth, at_ref, w_ref, mine_ref, rest_ref, tall):
    half = mine_ref.shape[1]
    tall[pl.ds(rows // 8 * 8, tall.shape[0] - rows // 8 * 8), :] = jnp.zeros(
        (tall.shape[0] - rows // 8 * 8, tall.shape[1]), jnp.float32
    )
    edge = depth // LANES * LANES
    tall[:, pl.ds(edge, tall.shape[1] - edge)] = jnp.zeros(
        (tall.shape[0], tall.shape[1] - edge), jnp.float32
    )
    for r in range(rows):
        tall[r : r + 1, 0:depth] = w_ref[0, :, depth * r : depth * (r + 1)].astype(jnp.float32)
    y = at_ref[0]
    mine_ref[...] = tall[:, pl.ds(pl.multiple_of(y * half, LANES), half)].astype(jnp.bfloat16)
    rest_ref[...] = tall[:, pl.ds(pl.multiple_of((1 - y) * half, LANES), half)].astype(jnp.bfloat16)


def head_mask():
    row = lax.broadcasted_iota(jnp.int32, (LANES, LANES), 0) // HD
    lane = lax.broadcasted_iota(jnp.int32, (LANES, LANES), 1) // HD
    return row == lane


def state_sums(half, at_ref, k_ref, v_ref, own_ref, other_ref, sums):
    depth = k_ref.shape[1]
    mask = head_mask()
    sums[...] = jnp.zeros_like(sums)
    for start in range(0, depth, LANES):
        n = min(LANES, depth - start)
        keys = jnp.maximum(k_ref[:, start : start + n], 0)
        values = v_ref[:, start : start + n]
        outer = lax.dot_general(
            values, keys, (((0,), (0,)), ((), ())), preferred_element_type=jnp.float32
        )
        outer = jnp.where(mask[:n, :n], outer, 0.0)
        folded = sum(outer[i : i + HD] for i in range(0, n, HD))
        sums[0:HD, start : start + n] = folded
        sums[HD : HD + 1, start : start + n] = jnp.sum(
            keys.astype(jnp.float32), axis=0, keepdims=True
        )
    own_ref[...] = jnp.zeros_like(own_ref)
    other_ref[...] = jnp.zeros_like(other_ref)

    @pl.when(at_ref[1] == 0)
    def _():
        own_ref[:, 0:half] = sums[:, 0:half]
        other_ref[:, 0:half] = sums[:, half : 2 * half]

    @pl.when(at_ref[1] != 0)
    def _():
        own_ref[:, 0:half] = sums[:, half : 2 * half]
        other_ref[:, 0:half] = sums[:, 0:half]


def read_states(half, shard, slots, at_ref, q_ref, p_ref, s_ref, g_ref, left_ref, square_ref, qh, gh, flat, blocks):
    count = q_ref.shape[0]
    qh[...] = jnp.zeros_like(qh)
    gh[...] = jnp.zeros_like(gh)

    def take(first):
        qh[0:count, 0:half] = q_ref[:, first : first + half]
        qh[count : 2 * count, 0:half] = p_ref[:, first : first + half]
        gh[:, 0:half] = g_ref[:, first : first + half]

    @pl.when(at_ref[1] == 0)
    def _():
        take(0)

    @pl.when(at_ref[1] != 0)
    def _():
        take(half)

    mask = head_mask()
    square = jnp.zeros((2 * count, LANES), jnp.float32)
    for start in range(0, qh.shape[1], LANES):
        query = jnp.maximum(qh[:, start : start + LANES], 0)
        state = s_ref[0:HD, start : start + LANES]
        total = s_ref[HD : HD + 1, start : start + LANES]
        spread = jnp.concatenate(
            [
                jnp.where(mask, jnp.concatenate([state] * (LANES // HD), axis=0), 0.0),
                jnp.where(mask, jnp.broadcast_to(total, (LANES, LANES)), 0.0),
            ],
            axis=0,
        )
        high = spread.astype(jnp.bfloat16)
        low = (spread - high.astype(jnp.float32)).astype(jnp.bfloat16)
        both = lax.dot_general(
            jnp.concatenate([query, query], axis=1),
            jnp.concatenate([high, low], axis=1),
            (((1,), (1,)), ((), ())),
            preferred_element_type=jnp.float32,
        )
        reads = both[:, 0:LANES] / (both[:, LANES : 2 * LANES] + read_epsilon)
        square += reads * reads
        flat[:, start : start + LANES] = (reads * gh[:, start : start + LANES]).astype(jnp.bfloat16)
    square_ref[...] = jnp.broadcast_to(
        jnp.sum(square, axis=1, keepdims=True), square_ref.shape
    )
    wide = left_ref.shape[1] // slots
    blocks[...] = jnp.zeros_like(blocks)
    for t in range(slots):
        blocks[t, :, 0:shard] = flat[:, shard * t : shard * (t + 1)]
    me = at_ref[2]
    for m in range(slots):
        left_ref[:, wide * m : wide * (m + 1)] = blocks[me ^ m]


def project(first, last, sides, spare, at_ref, left_ref, square_ref, *refs):
    refs = list(refs)
    out_ref = refs.pop()
    pieces = [[refs.pop(0) for _ in slots] for slots in sides]
    base = refs.pop(0) if refs else None
    wide = pieces[0][0].shape[0] if pieces[0] else pieces[1][0].shape[0]
    for i, slots in enumerate(sides):
        weight = jnp.concatenate([p[...] for p in pieces[i]], axis=0)
        left = jnp.concatenate(
            [left_ref[first:last, wide * m : wide * (m + 1)] for m in slots], axis=1
        )
        total = jnp.dot(left, weight, preferred_element_type=jnp.float32)
        out_ref[i] = total if base is None else total + base[i, first:last]
    if base is not None:
        tail = 1 - at_ref[0]
        lane = lax.broadcasted_iota(jnp.int32, (last - first, LANES), 1)
        cut = spare // LANES * LANES
        out_ref[tail, :, cut : cut + LANES] = jnp.where(
            lane == spare % LANES, square_ref[first:last], out_ref[tail, :, cut : cut + LANES]
        )


def finish(depth, spare, at_ref, own_ref, got_ref, out_ref):
    half = own_ref.shape[2]
    first, last = at_ref[0], 1 - at_ref[0]
    right = own_ref[last] + got_ref[last]
    scale = lax.rsqrt(right[:, spare : spare + 1] / depth + norm_epsilon)
    out_ref[:, half:depth] = (right[:, : depth - half] * scale).astype(jnp.bfloat16)
    out_ref[:, 0:half] = ((own_ref[first] + got_ref[first]) * scale).astype(jnp.bfloat16)


def fast(query_tokens, key_tokens, value_tokens, norm_gain, out_weight):
    frames, rows, width, depth = query_tokens.shape
    count = rows * width
    bands, peers = lax.axis_size("band"), lax.axis_size("tm")
    half = depth // bands
    wide = round_up(half, LANES)
    shard = out_weight.shape[-1] // depth
    tall = round_up(shard, 16)
    cols = round_up(depth, 2 * LANES) // 2
    spare = depth - cols
    swap = [(0, 1), (1, 0)]

    def flip(x, mask):
        return lax.ppermute(x, "tm", [(i, i ^ mask) for i in range(peers)])

    def across(x, axis):
        return lax.ppermute(x, axis, swap)

    at = jnp.stack(
        [lax.axis_index("parts"), lax.axis_index("band"), lax.axis_index("tm")]
    ).astype(jnp.int32)
    bf16, f32 = jnp.bfloat16, jnp.float32

    mine, rest = {}, {}
    mine[0], rest[0] = call(
        functools.partial(unpack_weight, shard, depth),
        (shape((tall, cols), bf16), shape((tall, cols), bf16)),
        (at, out_weight),
        scratch=[pltpu.VMEM((tall, 2 * cols), f32)],
        smem=1,
    )
    far = range(2, peers, 2)
    for m in far:
        mine[m] = flip(mine[0], m)
    mine[1], rest[1] = flip(mine[0], 1), flip(rest[0], 1)
    for m in far:
        mine[m + 1] = flip(mine[m], 1)
        rest[m] = across(mine[m], "parts")
    for m in far:
        if m == 2:
            rest[m + 1] = flip(rest[m], 1)
        else:
            rest[m + 1] = across(mine[m + 1], "parts")

    queries = query_tokens.reshape(count, depth)
    partner = across(query_tokens, "band").reshape(count, depth)
    own, other = call(
        functools.partial(state_sums, half),
        (shape((HD + 8, wide), f32), shape((HD + 8, wide), f32)),
        (at, key_tokens.reshape(count, depth), value_tokens.reshape(count, depth)),
        scratch=[pltpu.VMEM((HD + 8, round_up(depth, LANES)), f32)],
        smem=1,
        flops=2 * count * LANES * depth,
    )
    total = own + across(other, "band")
    prefix = total
    step = 0
    while 1 << step < peers:
        got = flip(total, 1 << step)
        prefix = prefix + jnp.where((at[2] & (1 << step)) != 0, got, 0.0)
        total = total + got
        step += 1
    left, square = call(
        functools.partial(read_states, half, shard, peers),
        (shape((2 * count, peers * tall), bf16), shape((2 * count, LANES), f32)),
        (at, queries, partner, prefix, norm_gain.reshape(1, depth)),
        scratch=[
            pltpu.VMEM((2 * count, wide), bf16),
            pltpu.VMEM((1, wide), f32),
            pltpu.VMEM((2 * count, wide), bf16),
            pltpu.VMEM((peers, 2 * count, tall), bf16),
        ],
        smem=1,
        flops=8 * count * LANES * wide,
    )

    def partial_sums(first, last, slots, base):
        sides = ((slots[0], mine), (slots[1], rest))
        pieces = [held[m] for chosen, held in sides for m in chosen]
        return call(
            functools.partial(project, first, last, slots, spare),
            shape((2, last - first, cols), f32),
            (at, left, square, *pieces, *base),
            smem=1,
            flops=2 * (last - first) * cols * tall * len(pieces),
        )

    late = ((peers - 1,), (peers - 2, peers - 1))
    soon = tuple(tuple(m for m in range(peers) if m not in side) for side in late)
    base = partial_sums(0, 2 * count, soon, ())
    other = partial_sums(count, 2 * count, late, (base,))
    own = partial_sums(0, count, late, (base,))
    out = call(
        functools.partial(finish, depth, spare),
        shape((count, depth), bf16),
        (at, own, across(other, "band")),
        smem=1,
    )
    return out.reshape(frames, rows, width, depth)


def entering(x, axis, combine, identity):
    peers, place = (lax.axis_size(axis), lax.axis_index(axis))
    everything = jax.tree.map(lambda part: lax.all_gather(part, axis), x)
    start = jax.tree.map(
        lambda part, zero: jnp.broadcast_to(jnp.asarray(zero, part.dtype), part.shape), x, identity
    )

    def hop(k, before):
        reached = k < place
        new = combine(before, jax.tree.map(lambda part: part[k], everything))
        return jax.tree.map(lambda a, b: jnp.where(reached, a, b), new, before)

    return lax.fori_loop(0, peers, hop, start)


def add_pair(earlier, later):
    return (earlier[0] + later[0], earlier[1] + later[1])


def general(query_tokens, key_tokens, value_tokens, norm_gain, out_weight):
    frames, rows, width, depth = query_tokens.shape
    key_relu = jax.nn.relu(key_tokens).reshape(frames, rows * width, HEADS, HD)
    value_heads = value_tokens.reshape(frames, rows * width, HEADS, HD)
    part_state = jnp.einsum(
        "fthd,fthe->fhde", key_relu, value_heads, preferred_element_type=jnp.float32
    ).reshape(frames, HEADS, HD * HD)
    part_norm = jnp.sum(key_relu, axis=1, dtype=jnp.float32)
    state_sum, norm_sum = lax.psum((part_state, part_norm), "band")
    local_state = jnp.cumsum(state_sum, axis=0)
    local_norm = jnp.cumsum(norm_sum, axis=0)
    before = entering(
        (local_state[-1], local_norm[-1]),
        "tm",
        add_pair,
        (jnp.zeros_like(local_state[-1]), jnp.zeros_like(local_norm[-1])),
    )
    prefix_state = local_state + before[0]
    prefix_norm = local_norm + before[1]
    query_relu = jax.nn.relu(query_tokens.astype(jnp.float32)).reshape(
        frames, rows * width, HEADS, HD
    )
    numer = jnp.einsum(
        "fthd,fhde->fthe",
        query_relu,
        prefix_state.reshape(frames, HEADS, HD, HD),
        precision=lax.Precision.HIGHEST,
    )
    denom = (
        jnp.einsum("fthd,fhd->fth", query_relu, prefix_norm, precision=lax.Precision.HIGHEST)
        + read_epsilon
    )
    reads = (numer / denom[:, :, :, None]).reshape(frames * rows * width, depth)
    square = jnp.mean(reads * reads, axis=-1, keepdims=True)
    normed = (reads * lax.rsqrt(square + norm_epsilon) * norm_gain).astype(jnp.bfloat16)
    gathered = lax.all_gather(out_weight, "tm", axis=1, tiled=True)
    rows_half = gathered.reshape(-1, depth)
    result = jnp.dot(
        normed,
        lax.all_gather(rows_half, "band", axis=0, tiled=True),
        preferred_element_type=jnp.float32,
    )
    return result.astype(jnp.bfloat16).reshape(frames, rows, width, depth)


def body(query_tokens, key_tokens, value_tokens, norm_gain, out_weight):
    frames, depth = query_tokens.shape[0], query_tokens.shape[-1]
    peers = lax.axis_size("tm")
    whole_rows = (
        frames == 1
        and lax.axis_size("band") == 2
        and lax.axis_size("parts") == 2
        and peers > 1
        and peers & (peers - 1) == 0
        and out_weight.shape[-1] % depth == 0
        and depth % (2 * HD) == 0
        and round_up(depth, 2 * LANES) > depth
    )
    run = fast if whole_rows else general
    return run(query_tokens, key_tokens, value_tokens, norm_gain, out_weight)


def solution(mesh):
    in_specs = (
        P(("parts", "tm"), "band", None, None),
        P(("parts", "tm"), "band", None, None),
        P(("parts", "tm"), "band", None, None),
        P(),
        P("band", "tm", None),
    )
    out_specs = P(("parts", "tm"), "band", None, None)
    return jax.shard_map(body, mesh=mesh, in_specs=in_specs, out_specs=out_specs, check_vma=False)
```

```python
import functools

import jax
import jax.numpy as jnp
from jax import lax
from jax.experimental import pallas as pl
from jax.experimental.pallas import tpu as pltpu
from jax.sharding import PartitionSpec as P


HEADS = 70
HD = 32
LANES = 128

norm_epsilon = 1e-06
read_epsilon = 1e-06


def round_up(n, m):
    return -(-n // m) * m


def call(kernel, out, args, scratch=(), flops=0, smem=0, mib=16):
    whole = pl.BlockSpec(memory_space=pltpu.VMEM)
    scalar = pl.BlockSpec(memory_space=pltpu.SMEM)
    moved = sum(a.size * a.dtype.itemsize for a in jax.tree.leaves((args, out)))
    return pl.pallas_call(
        kernel,
        out_shape=out,
        in_specs=[scalar] * smem + [whole] * (len(args) - smem),
        out_specs=jax.tree.map(lambda _: whole, out),
        scratch_shapes=list(scratch),
        compiler_params=pltpu.CompilerParams(vmem_limit_bytes=mib * 1024 * 1024),
        cost_estimate=pl.CostEstimate(flops=flops, bytes_accessed=moved, transcendentals=0),
    )(*args)


def line_ring(length):
    return [0, *range(1, length, 2), *reversed(range(2, length, 2))]


def ring_place(z, length):
    return jnp.where(z % 2 == 1, (z + 1) // 2, jnp.where(z == 0, 0, length - z // 2))


def at_ring_place(p, length):
    return jnp.where(p == 0, 0, jnp.where(p <= length // 2, 2 * p - 1, 2 * (length - p)))


def shape(dims, dtype):
    return jax.ShapeDtypeStruct(tuple(dims), dtype)


def unpack_weight(rows, depth, at_ref, w_ref, mine_ref, both_ref, tall):
    half = mine_ref.shape[1]
    tall[pl.ds(rows // 8 * 8, tall.shape[0] - rows // 8 * 8), :] = jnp.zeros(
        (tall.shape[0] - rows // 8 * 8, tall.shape[1]), jnp.float32
    )
    edge = depth // LANES * LANES
    tall[:, pl.ds(edge, tall.shape[1] - edge)] = jnp.zeros(
        (tall.shape[0], tall.shape[1] - edge), jnp.float32
    )
    for r in range(rows):
        tall[r : r + 1, 0:depth] = w_ref[0, :, depth * r : depth * (r + 1)].astype(jnp.float32)
    y = at_ref[0]
    first = tall[:, pl.ds(pl.multiple_of(y * half, LANES), half)].astype(jnp.bfloat16)
    mine_ref[...] = first
    both_ref[0] = first
    both_ref[1] = tall[:, pl.ds(pl.multiple_of((1 - y) * half, LANES), half)].astype(jnp.bfloat16)


def head_mask():
    row = lax.broadcasted_iota(jnp.int32, (LANES, LANES), 0) // HD
    lane = lax.broadcasted_iota(jnp.int32, (LANES, LANES), 1) // HD
    return row == lane


def state_sums(half, at_ref, k_ref, v_ref, own_ref, other_ref, sums):
    depth = k_ref.shape[1]
    mask = head_mask()
    sums[...] = jnp.zeros_like(sums)
    for start in range(0, depth, LANES):
        n = min(LANES, depth - start)
        keys = jnp.maximum(k_ref[:, start : start + n], 0)
        values = v_ref[:, start : start + n]
        outer = lax.dot_general(
            values, keys, (((0,), (0,)), ((), ())), preferred_element_type=jnp.float32
        )
        outer = jnp.where(mask[:n, :n], outer, 0.0)
        folded = sum(outer[i : i + HD] for i in range(0, n, HD))
        sums[0:HD, start : start + n] = folded
        sums[HD : HD + 1, start : start + n] = jnp.sum(
            keys.astype(jnp.float32), axis=0, keepdims=True
        )
    own_ref[...] = jnp.zeros_like(own_ref)
    other_ref[...] = jnp.zeros_like(other_ref)

    @pl.when(at_ref[1] == 0)
    def _():
        own_ref[:, 0:half] = sums[:, 0:half]
        other_ref[:, 0:half] = sums[:, half : 2 * half]

    @pl.when(at_ref[1] != 0)
    def _():
        own_ref[:, 0:half] = sums[:, half : 2 * half]
        other_ref[:, 0:half] = sums[:, 0:half]


def read_states(half, shard, slots, at_ref, q_ref, p_ref, s_ref, g_ref, left_ref, square_ref, qh, gh, flat, blocks):
    count = q_ref.shape[0]
    qh[...] = jnp.zeros_like(qh)
    gh[...] = jnp.zeros_like(gh)

    def take(first):
        qh[0:count, 0:half] = q_ref[:, first : first + half]
        qh[count : 2 * count, 0:half] = p_ref[:, first : first + half]
        gh[:, 0:half] = g_ref[:, first : first + half]

    @pl.when(at_ref[1] == 0)
    def _():
        take(0)

    @pl.when(at_ref[1] != 0)
    def _():
        take(half)

    mask = head_mask()
    square = jnp.zeros((2 * count, LANES), jnp.float32)
    for start in range(0, qh.shape[1], LANES):
        query = jnp.maximum(qh[:, start : start + LANES], 0)
        state = s_ref[0:HD, start : start + LANES]
        total = s_ref[HD : HD + 1, start : start + LANES]
        spread = jnp.concatenate(
            [
                jnp.where(mask, jnp.concatenate([state] * (LANES // HD), axis=0), 0.0),
                jnp.where(mask, jnp.broadcast_to(total, (LANES, LANES)), 0.0),
            ],
            axis=0,
        )
        high = spread.astype(jnp.bfloat16)
        low = (spread - high.astype(jnp.float32)).astype(jnp.bfloat16)
        both = lax.dot_general(
            jnp.concatenate([query, query], axis=1),
            jnp.concatenate([high, low], axis=1),
            (((1,), (1,)), ((), ())),
            preferred_element_type=jnp.float32,
        )
        reads = both[:, 0:LANES] / (both[:, LANES : 2 * LANES] + read_epsilon)
        square += reads * reads
        flat[:, start : start + LANES] = (reads * gh[:, start : start + LANES]).astype(jnp.bfloat16)
    square_ref[...] = jnp.broadcast_to(
        jnp.sum(square, axis=1, keepdims=True), square_ref.shape
    )
    wide = left_ref.shape[1] // slots
    blocks[...] = jnp.zeros_like(blocks)
    for t in range(slots):
        blocks[t, :, 0:shard] = flat[:, shard * t : shard * (t + 1)]
    length = slots // 2
    z, x = at_ref[2] // 2, at_ref[2] % 2
    place = ring_place(z, length)
    for m in range(slots):
        source = at_ring_place((place + length - m // 2) % length, length)
        left_ref[:, wide * m : wide * (m + 1)] = blocks[2 * source + (x ^ (m % 2))]


def project(first, last, sides, plan, spare, at_ref, left_ref, square_ref, *refs):
    refs = list(refs)
    out_ref = refs.pop()
    count = 1 + max(at for pieces in plan for at, _ in pieces)
    base = refs[count] if len(refs) > count else None
    pieces = [
        [refs[at][...] if part is None else refs[at][part] for at, part in side] for side in plan
    ]
    wide = (pieces[0] + pieces[1])[0].shape[0]
    for i, slots in enumerate(sides):
        weight = jnp.concatenate(pieces[i], axis=0)
        left = jnp.concatenate(
            [left_ref[first:last, wide * m : wide * (m + 1)] for m in slots], axis=1
        )
        total = jnp.dot(left, weight, preferred_element_type=jnp.float32)
        out_ref[i] = total if base is None else total + base[i, first:last]
    if base is not None:
        tail = 1 - at_ref[0]
        lane = lax.broadcasted_iota(jnp.int32, (last - first, LANES), 1)
        cut = spare // LANES * LANES
        out_ref[tail, :, cut : cut + LANES] = jnp.where(
            lane == spare % LANES, square_ref[first:last], out_ref[tail, :, cut : cut + LANES]
        )


def finish(depth, spare, at_ref, own_ref, got_ref, out_ref):
    half = own_ref.shape[2]
    first, last = at_ref[0], 1 - at_ref[0]
    right = own_ref[last] + got_ref[last]
    scale = lax.rsqrt(right[:, spare : spare + 1] / depth + norm_epsilon)
    out_ref[:, half:depth] = (right[:, : depth - half] * scale).astype(jnp.bfloat16)
    out_ref[:, 0:half] = ((own_ref[first] + got_ref[first]) * scale).astype(jnp.bfloat16)


def fast(query_tokens, key_tokens, value_tokens, norm_gain, out_weight):
    frames, rows, width, depth = query_tokens.shape
    count = rows * width
    bands, peers = lax.axis_size("band"), lax.axis_size("tm")
    half = depth // bands
    wide = round_up(half, LANES)
    shard = out_weight.shape[-1] // depth
    tall = round_up(shard, 16)
    cols = round_up(depth, 2 * LANES) // 2
    spare = depth - cols
    swap = [(0, 1), (1, 0)]

    def flip(x, mask):
        return lax.ppermute(x, "tm", [(i, i ^ mask) for i in range(peers)])

    def across(x, axis):
        return lax.ppermute(x, axis, swap)

    at = jnp.stack(
        [lax.axis_index("parts"), lax.axis_index("band"), lax.axis_index("tm")]
    ).astype(jnp.int32)
    bf16, f32 = jnp.bfloat16, jnp.float32

    mine, rest = {}, {}
    mine[0], both = call(
        functools.partial(unpack_weight, shard, depth),
        (shape((tall, cols), bf16), shape((2, tall, cols), bf16)),
        (at, out_weight),
        scratch=[pltpu.VMEM((tall, 2 * cols), f32)],
        smem=1,
    )
    length = peers // 2
    order = line_ring(length)
    onward = [
        (2 * a + x, 2 * b + x) for a, b in zip(order, order[1:] + order[:1]) for x in range(2)
    ]
    beside = flip(both, 1)
    rest[0] = (both, 1)
    mine[1], rest[1] = (beside, 0), (beside, 1)
    for k in range(1, length):
        m = 2 * k
        mine[m] = lax.ppermute(mine[m - 2], "tm", onward)
        rest[m] = across(mine[m], "parts")
        if k < length - 1:
            last = beside[0] if k == 1 else mine[m - 1]
            mine[m + 1] = lax.ppermute(last, "tm", onward)
            rest[m + 1] = flip(rest[m], 1)
        else:
            mine[m + 1] = flip(mine[m], 1)
            rest[m + 1] = across(mine[m + 1], "parts")

    queries = query_tokens.reshape(count, depth)
    partner = across(query_tokens, "band").reshape(count, depth)
    own, other = call(
        functools.partial(state_sums, half),
        (shape((HD + 8, wide), f32), shape((HD + 8, wide), f32)),
        (at, key_tokens.reshape(count, depth), value_tokens.reshape(count, depth)),
        scratch=[pltpu.VMEM((HD + 8, round_up(depth, LANES)), f32)],
        smem=1,
        flops=2 * count * LANES * depth,
    )
    total = own + across(other, "band")
    sent = total.astype(bf16)
    prefix = total
    step = 0
    while 1 << step < peers:
        got = flip(sent, 1 << step)
        prefix = prefix + jnp.where((at[2] & (1 << step)) != 0, got.astype(f32), 0.0)
        total = total + got.astype(f32)
        sent = total.astype(bf16)
        step += 1
    left, square = call(
        functools.partial(read_states, half, shard, peers),
        (shape((2 * count, peers * tall), bf16), shape((2 * count, LANES), f32)),
        (at, queries, partner, prefix, norm_gain.reshape(1, depth)),
        scratch=[
            pltpu.VMEM((2 * count, wide), bf16),
            pltpu.VMEM((1, wide), f32),
            pltpu.VMEM((2 * count, wide), bf16),
            pltpu.VMEM((peers, 2 * count, tall), bf16),
        ],
        smem=1,
        flops=8 * count * LANES * wide,
    )

    def partial_sums(first, last, slots, base):
        arrays, plan = [], []
        for chosen, held in zip(slots, (mine, rest)):
            plan.append([])
            for m in chosen:
                array, part = held[m] if isinstance(held[m], tuple) else (held[m], None)
                if not any(array is a for a in arrays):
                    arrays.append(array)
                plan[-1].append(([array is a for a in arrays].index(True), part))
        return call(
            functools.partial(project, first, last, slots, plan, spare),
            shape((2, last - first, cols), f32),
            (at, left, square, *arrays, *base),
            smem=1,
            flops=2 * (last - first) * cols * tall * sum(map(len, plan)),
        )

    late = ((peers - 3,), (peers - 3, peers - 1))
    soon = tuple(tuple(m for m in range(peers) if m not in side) for side in late)
    base = partial_sums(0, 2 * count, soon, ())
    other = partial_sums(count, 2 * count, late, (base,))
    own = partial_sums(0, count, late, (base,))
    out = call(
        functools.partial(finish, depth, spare),
        shape((count, depth), bf16),
        (at, own, across(other, "band")),
        smem=1,
    )
    return out.reshape(frames, rows, width, depth)


def entering(x, axis, combine, identity):
    peers, place = (lax.axis_size(axis), lax.axis_index(axis))
    everything = jax.tree.map(lambda part: lax.all_gather(part, axis), x)
    start = jax.tree.map(
        lambda part, zero: jnp.broadcast_to(jnp.asarray(zero, part.dtype), part.shape), x, identity
    )

    def hop(k, before):
        reached = k < place
        new = combine(before, jax.tree.map(lambda part: part[k], everything))
        return jax.tree.map(lambda a, b: jnp.where(reached, a, b), new, before)

    return lax.fori_loop(0, peers, hop, start)


def add_pair(earlier, later):
    return (earlier[0] + later[0], earlier[1] + later[1])


def general(query_tokens, key_tokens, value_tokens, norm_gain, out_weight):
    frames, rows, width, depth = query_tokens.shape
    key_relu = jax.nn.relu(key_tokens).reshape(frames, rows * width, HEADS, HD)
    value_heads = value_tokens.reshape(frames, rows * width, HEADS, HD)
    part_state = jnp.einsum(
        "fthd,fthe->fhde", key_relu, value_heads, preferred_element_type=jnp.float32
    ).reshape(frames, HEADS, HD * HD)
    part_norm = jnp.sum(key_relu, axis=1, dtype=jnp.float32)
    state_sum, norm_sum = lax.psum((part_state, part_norm), "band")
    local_state = jnp.cumsum(state_sum, axis=0)
    local_norm = jnp.cumsum(norm_sum, axis=0)
    before = entering(
        (local_state[-1], local_norm[-1]),
        "tm",
        add_pair,
        (jnp.zeros_like(local_state[-1]), jnp.zeros_like(local_norm[-1])),
    )
    prefix_state = local_state + before[0]
    prefix_norm = local_norm + before[1]
    query_relu = jax.nn.relu(query_tokens.astype(jnp.float32)).reshape(
        frames, rows * width, HEADS, HD
    )
    numer = jnp.einsum(
        "fthd,fhde->fthe",
        query_relu,
        prefix_state.reshape(frames, HEADS, HD, HD),
        precision=lax.Precision.HIGHEST,
    )
    denom = (
        jnp.einsum("fthd,fhd->fth", query_relu, prefix_norm, precision=lax.Precision.HIGHEST)
        + read_epsilon
    )
    reads = (numer / denom[:, :, :, None]).reshape(frames * rows * width, depth)
    square = jnp.mean(reads * reads, axis=-1, keepdims=True)
    normed = (reads * lax.rsqrt(square + norm_epsilon) * norm_gain).astype(jnp.bfloat16)
    gathered = lax.all_gather(out_weight, "tm", axis=1, tiled=True)
    rows_half = gathered.reshape(-1, depth)
    result = jnp.dot(
        normed,
        lax.all_gather(rows_half, "band", axis=0, tiled=True),
        preferred_element_type=jnp.float32,
    )
    return result.astype(jnp.bfloat16).reshape(frames, rows, width, depth)


def body(query_tokens, key_tokens, value_tokens, norm_gain, out_weight):
    frames, depth = query_tokens.shape[0], query_tokens.shape[-1]
    peers = lax.axis_size("tm")
    whole_rows = (
        frames == 1
        and lax.axis_size("band") == 2
        and lax.axis_size("parts") == 2
        and peers > 2
        and peers & (peers - 1) == 0
        and out_weight.shape[-1] % depth == 0
        and depth % (2 * HD) == 0
        and round_up(depth, 2 * LANES) > depth
    )
    run = fast if whole_rows else general
    return run(query_tokens, key_tokens, value_tokens, norm_gain, out_weight)


def solution(mesh):
    in_specs = (
        P(("parts", "tm"), "band", None, None),
        P(("parts", "tm"), "band", None, None),
        P(("parts", "tm"), "band", None, None),
        P(),
        P("band", "tm", None),
    )
    out_specs = P(("parts", "tm"), "band", None, None)
    return jax.shard_map(body, mesh=mesh, in_specs=in_specs, out_specs=out_specs, check_vma=False)
```

```python
import functools

import jax
import jax.numpy as jnp
from jax import lax
from jax.experimental import pallas as pl
from jax.experimental.pallas import tpu as pltpu
from jax.sharding import PartitionSpec as P


HEADS = 70
HD = 32
LANES = 128

norm_epsilon = 1e-06
read_epsilon = 1e-06


def round_up(n, m):
    return -(-n // m) * m


def call(kernel, out, args, scratch=(), flops=0, smem=0, mib=16):
    whole = pl.BlockSpec(memory_space=pltpu.VMEM)
    scalar = pl.BlockSpec(memory_space=pltpu.SMEM)
    moved = sum(a.size * a.dtype.itemsize for a in jax.tree.leaves((args, out)))
    return pl.pallas_call(
        kernel,
        out_shape=out,
        in_specs=[scalar] * smem + [whole] * (len(args) - smem),
        out_specs=jax.tree.map(lambda _: whole, out),
        scratch_shapes=list(scratch),
        compiler_params=pltpu.CompilerParams(vmem_limit_bytes=mib * 1024 * 1024),
        cost_estimate=pl.CostEstimate(flops=flops, bytes_accessed=moved, transcendentals=0),
    )(*args)


def line_ring(length):
    return [0, *range(1, length, 2), *reversed(range(2, length, 2))]


def ring_place(z, length):
    return jnp.where(z % 2 == 1, (z + 1) // 2, jnp.where(z == 0, 0, length - z // 2))


def at_ring_place(p, length):
    return jnp.where(p == 0, 0, jnp.where(p <= length // 2, 2 * p - 1, 2 * (length - p)))


def shape(dims, dtype):
    return jax.ShapeDtypeStruct(tuple(dims), dtype)


def unpack_weight(rows, depth, at_ref, w_ref, mine_ref, both_ref, tall):
    half = mine_ref.shape[1]
    tall[pl.ds(rows // 8 * 8, tall.shape[0] - rows // 8 * 8), :] = jnp.zeros(
        (tall.shape[0] - rows // 8 * 8, tall.shape[1]), jnp.float32
    )
    edge = depth // LANES * LANES
    tall[:, pl.ds(edge, tall.shape[1] - edge)] = jnp.zeros(
        (tall.shape[0], tall.shape[1] - edge), jnp.float32
    )
    for r in range(rows):
        tall[r : r + 1, 0:depth] = w_ref[0, :, depth * r : depth * (r + 1)].astype(jnp.float32)
    y = at_ref[0]
    first = tall[:, pl.ds(pl.multiple_of(y * half, LANES), half)].astype(jnp.bfloat16)
    mine_ref[...] = first
    both_ref[0] = first
    both_ref[1] = tall[:, pl.ds(pl.multiple_of((1 - y) * half, LANES), half)].astype(jnp.bfloat16)


def head_mask():
    row = lax.broadcasted_iota(jnp.int32, (LANES, LANES), 0) // HD
    lane = lax.broadcasted_iota(jnp.int32, (LANES, LANES), 1) // HD
    return row == lane


def state_sums(half, at_ref, k_ref, v_ref, own_ref, other_ref, sums):
    depth = k_ref.shape[1]
    mask = head_mask()
    sums[...] = jnp.zeros_like(sums)
    for start in range(0, depth, LANES):
        n = min(LANES, depth - start)
        keys = jnp.maximum(k_ref[:, start : start + n], 0)
        values = v_ref[:, start : start + n]
        outer = lax.dot_general(
            values, keys, (((0,), (0,)), ((), ())), preferred_element_type=jnp.float32
        )
        outer = jnp.where(mask[:n, :n], outer, 0.0)
        folded = sum(outer[i : i + HD] for i in range(0, n, HD))
        sums[0:HD, start : start + n] = folded
        sums[HD : HD + 1, start : start + n] = jnp.sum(
            keys.astype(jnp.float32), axis=0, keepdims=True
        )
    own_ref[...] = jnp.zeros_like(own_ref)
    other_ref[...] = jnp.zeros_like(other_ref)

    @pl.when(at_ref[1] == 0)
    def _():
        own_ref[:, 0:half] = sums[:, 0:half]
        other_ref[:, 0:half] = sums[:, half : 2 * half]

    @pl.when(at_ref[1] != 0)
    def _():
        own_ref[:, 0:half] = sums[:, half : 2 * half]
        other_ref[:, 0:half] = sums[:, 0:half]


def read_states(half, shard, slots, at_ref, q_ref, p_ref, g_ref, total_ref, *refs):
    steps = slots.bit_length() - 1
    scanned = refs[:steps]
    left_ref, square_ref, qh, gh, flat, blocks, s_ref = refs[steps:]
    s_ref[...] = total_ref[...]
    for step, got in enumerate(scanned):
        reached = (at_ref[2] >> step) % 2 == 1
        s_ref[...] += jnp.where(reached, got[...].astype(jnp.float32), 0.0)
    count = q_ref.shape[0]
    qh[...] = jnp.zeros_like(qh)
    gh[...] = jnp.zeros_like(gh)

    def take(first):
        qh[0:count, 0:half] = q_ref[:, first : first + half]
        qh[count : 2 * count, 0:half] = p_ref[:, first : first + half]
        gh[:, 0:half] = g_ref[:, first : first + half]

    @pl.when(at_ref[1] == 0)
    def _():
        take(0)

    @pl.when(at_ref[1] != 0)
    def _():
        take(half)

    mask = head_mask()
    square = jnp.zeros((2 * count, LANES), jnp.float32)
    for start in range(0, qh.shape[1], LANES):
        query = jnp.maximum(qh[:, start : start + LANES], 0)
        state = s_ref[0:HD, start : start + LANES]
        total = s_ref[HD : HD + 1, start : start + LANES]
        spread = jnp.concatenate(
            [
                jnp.where(mask, jnp.concatenate([state] * (LANES // HD), axis=0), 0.0),
                jnp.where(mask, jnp.broadcast_to(total, (LANES, LANES)), 0.0),
            ],
            axis=0,
        )
        high = spread.astype(jnp.bfloat16)
        low = (spread - high.astype(jnp.float32)).astype(jnp.bfloat16)
        both = lax.dot_general(
            jnp.concatenate([query, query], axis=1),
            jnp.concatenate([high, low], axis=1),
            (((1,), (1,)), ((), ())),
            preferred_element_type=jnp.float32,
        )
        reads = both[:, 0:LANES] / (both[:, LANES : 2 * LANES] + read_epsilon)
        square += reads * reads
        flat[:, start : start + LANES] = (reads * gh[:, start : start + LANES]).astype(jnp.bfloat16)
    square_ref[...] = jnp.broadcast_to(
        jnp.sum(square, axis=1, keepdims=True), square_ref.shape
    )
    wide = left_ref.shape[1] // slots
    blocks[...] = jnp.zeros_like(blocks)
    for t in range(slots):
        blocks[t, :, 0:shard] = flat[:, shard * t : shard * (t + 1)]
    length = slots // 2
    z, x = at_ref[2] // 2, at_ref[2] % 2
    place = ring_place(z, length)
    for m in range(slots):
        source = at_ring_place((place + length - m // 2) % length, length)
        left_ref[:, wide * m : wide * (m + 1)] = blocks[2 * source + (x ^ (m % 2))]


def product(left_ref, first, last, slots, pieces):
    weight = jnp.concatenate(
        [ref[...] if part is None else ref[part] for ref, part in pieces], axis=0
    )
    wide = weight.shape[0] // len(slots)
    left = jnp.concatenate(
        [left_ref[first:last, wide * m : wide * (m + 1)] for m in slots], axis=1
    )
    return jnp.dot(left, weight, preferred_element_type=jnp.float32)


def project_early(sides, plan, left_ref, *refs):
    outs = refs[-4:]
    count = outs[0].shape[0]
    for i, slots in enumerate(sides):
        pieces = [(refs[place], part) for place, part in plan[i]]
        total = product(left_ref, 0, 2 * count, slots, pieces)
        outs[2 * i][...] = total[:count]
        outs[2 * i + 1][...] = total[count:]


def project_late(first, last, slots, left_ref, base_ref, *refs):
    out_ref = refs[-1]
    pieces = [(ref, None) for ref in refs[:-1]]
    total = base_ref[...] + product(left_ref, first, last, slots, pieces)
    out_ref[...] = total.astype(out_ref.dtype)


def finish(depth, at_ref, square_ref, near_ref, mine_ref, got_mine_ref, rest_ref, got_rest_ref, out_ref):
    count, half = mine_ref.shape
    square = square_ref[0:count, 0:1] + near_ref[:, 0:1]
    scale = lax.rsqrt(square / depth + norm_epsilon)
    mine = ((mine_ref[...] + got_mine_ref[...].astype(jnp.float32)) * scale).astype(jnp.bfloat16)
    rest = ((rest_ref[...] + got_rest_ref[...].astype(jnp.float32)) * scale).astype(jnp.bfloat16)

    @pl.when(at_ref[0] == 0)
    def _():
        out_ref[:, 0:half] = mine
        out_ref[:, half:depth] = rest[:, : depth - half]

    @pl.when(at_ref[0] != 0)
    def _():
        out_ref[:, 0:half] = rest
        out_ref[:, half:depth] = mine[:, : depth - half]


def fast(query_tokens, key_tokens, value_tokens, norm_gain, out_weight):
    frames, rows, width, depth = query_tokens.shape
    count = rows * width
    bands, peers = lax.axis_size("band"), lax.axis_size("tm")
    half = depth // bands
    wide = round_up(half, LANES)
    shard = out_weight.shape[-1] // depth
    tall = round_up(shard, 16)
    cols = round_up(depth, 2 * LANES) // 2
    swap = [(0, 1), (1, 0)]

    def flip(x, mask):
        return lax.ppermute(x, "tm", [(i, i ^ mask) for i in range(peers)])

    def across(x, axis):
        return lax.ppermute(x, axis, swap)

    at = jnp.stack(
        [lax.axis_index("parts"), lax.axis_index("band"), lax.axis_index("tm")]
    ).astype(jnp.int32)
    bf16, f32 = jnp.bfloat16, jnp.float32

    mine, rest = {}, {}
    mine[0], both = call(
        functools.partial(unpack_weight, shard, depth),
        (shape((tall, cols), bf16), shape((2, tall, cols), bf16)),
        (at, out_weight),
        scratch=[pltpu.VMEM((tall, 2 * cols), f32)],
        smem=1,
    )
    length = peers // 2
    order = line_ring(length)
    onward = [
        (2 * a + x, 2 * b + x) for a, b in zip(order, order[1:] + order[:1]) for x in range(2)
    ]
    beside = flip(both, 1)
    rest[0] = (both, 1)
    mine[1], rest[1] = (beside, 0), (beside, 1)
    for k in range(1, length):
        m = 2 * k
        mine[m] = lax.ppermute(mine[m - 2], "tm", onward)
        rest[m] = across(mine[m], "parts")
        if k < length - 1:
            last = beside[0] if k == 1 else mine[m - 1]
            mine[m + 1] = lax.ppermute(last, "tm", onward)
            rest[m + 1] = flip(rest[m], 1)
        else:
            mine[m + 1] = flip(mine[m], 1)
            rest[m + 1] = across(mine[m + 1], "parts")

    queries = query_tokens.reshape(count, depth)
    partner = across(query_tokens, "band").reshape(count, depth)
    own, other = call(
        functools.partial(state_sums, half),
        (shape((HD + 8, wide), f32), shape((HD + 8, wide), f32)),
        (at, key_tokens.reshape(count, depth), value_tokens.reshape(count, depth)),
        scratch=[pltpu.VMEM((HD + 8, round_up(depth, LANES)), f32)],
        smem=1,
        flops=2 * count * LANES * depth,
    )
    total = own + across(other, "band")
    sent = total.astype(bf16)
    running, scanned = total, []
    while 1 << len(scanned) < peers:
        step = len(scanned)
        scanned.append(flip(sent, 1 << step))
        running = running + scanned[-1].astype(f32)
        sent = running.astype(bf16)
    left, square = call(
        functools.partial(read_states, half, shard, peers),
        (shape((2 * count, peers * tall), bf16), shape((2 * count, LANES), f32)),
        (at, queries, partner, norm_gain.reshape(1, depth), total, *scanned),
        scratch=[
            pltpu.VMEM((2 * count, wide), bf16),
            pltpu.VMEM((1, wide), f32),
            pltpu.VMEM((2 * count, wide), bf16),
            pltpu.VMEM((peers, 2 * count, tall), bf16),
            pltpu.VMEM((HD + 8, wide), f32),
        ],
        smem=1,
        flops=8 * count * LANES * wide,
    )

    near_square = across(square[count:], "band")
    late = ((peers - 3,), (peers - 3, peers - 1))
    soon = tuple(tuple(m for m in range(peers) if m not in side) for side in late)
    arrays, plan = [], []
    for chosen, held in zip(soon, (mine, rest)):
        plan.append([])
        for m in chosen:
            array, part = held[m] if isinstance(held[m], tuple) else (held[m], None)
            if not any(array is a for a in arrays):
                arrays.append(array)
            plan[-1].append(([array is a for a in arrays].index(True), part))
    base = call(
        functools.partial(project_early, soon, plan),
        (shape((count, cols), f32),) * 4,
        (left, *arrays),
        flops=4 * count * cols * tall * sum(map(len, plan)),
    )

    def finished(side, held):
        first = 2 * side
        sums = []
        for which, rows_from, dtype in (("other", count, bf16), ("own", 0, f32)):
            sums.append(
                call(
                    functools.partial(project_late, rows_from, rows_from + count, late[side]),
                    shape((count, cols), dtype),
                    (left, base[first + (which == "other")], *[held[m] for m in late[side]]),
                    flops=2 * count * cols * tall * len(late[side]),
                )
            )
        return sums[1], across(sums[0], "band")

    from_rest = finished(1, rest)
    from_mine = finished(0, mine)
    out = call(
        functools.partial(finish, depth),
        shape((count, depth), bf16),
        (at, square, near_square, *from_mine, *from_rest),
        smem=1,
    )
    return out.reshape(frames, rows, width, depth)


def entering(x, axis, combine, identity):
    peers, place = (lax.axis_size(axis), lax.axis_index(axis))
    everything = jax.tree.map(lambda part: lax.all_gather(part, axis), x)
    start = jax.tree.map(
        lambda part, zero: jnp.broadcast_to(jnp.asarray(zero, part.dtype), part.shape), x, identity
    )

    def hop(k, before):
        reached = k < place
        new = combine(before, jax.tree.map(lambda part: part[k], everything))
        return jax.tree.map(lambda a, b: jnp.where(reached, a, b), new, before)

    return lax.fori_loop(0, peers, hop, start)


def add_pair(earlier, later):
    return (earlier[0] + later[0], earlier[1] + later[1])


def general(query_tokens, key_tokens, value_tokens, norm_gain, out_weight):
    frames, rows, width, depth = query_tokens.shape
    key_relu = jax.nn.relu(key_tokens).reshape(frames, rows * width, HEADS, HD)
    value_heads = value_tokens.reshape(frames, rows * width, HEADS, HD)
    part_state = jnp.einsum(
        "fthd,fthe->fhde", key_relu, value_heads, preferred_element_type=jnp.float32
    ).reshape(frames, HEADS, HD * HD)
    part_norm = jnp.sum(key_relu, axis=1, dtype=jnp.float32)
    state_sum, norm_sum = lax.psum((part_state, part_norm), "band")
    local_state = jnp.cumsum(state_sum, axis=0)
    local_norm = jnp.cumsum(norm_sum, axis=0)
    before = entering(
        (local_state[-1], local_norm[-1]),
        "tm",
        add_pair,
        (jnp.zeros_like(local_state[-1]), jnp.zeros_like(local_norm[-1])),
    )
    prefix_state = local_state + before[0]
    prefix_norm = local_norm + before[1]
    query_relu = jax.nn.relu(query_tokens.astype(jnp.float32)).reshape(
        frames, rows * width, HEADS, HD
    )
    numer = jnp.einsum(
        "fthd,fhde->fthe",
        query_relu,
        prefix_state.reshape(frames, HEADS, HD, HD),
        precision=lax.Precision.HIGHEST,
    )
    denom = (
        jnp.einsum("fthd,fhd->fth", query_relu, prefix_norm, precision=lax.Precision.HIGHEST)
        + read_epsilon
    )
    reads = (numer / denom[:, :, :, None]).reshape(frames * rows * width, depth)
    square = jnp.mean(reads * reads, axis=-1, keepdims=True)
    normed = (reads * lax.rsqrt(square + norm_epsilon) * norm_gain).astype(jnp.bfloat16)
    gathered = lax.all_gather(out_weight, "tm", axis=1, tiled=True)
    rows_half = gathered.reshape(-1, depth)
    result = jnp.dot(
        normed,
        lax.all_gather(rows_half, "band", axis=0, tiled=True),
        preferred_element_type=jnp.float32,
    )
    return result.astype(jnp.bfloat16).reshape(frames, rows, width, depth)


def body(query_tokens, key_tokens, value_tokens, norm_gain, out_weight):
    frames, depth = query_tokens.shape[0], query_tokens.shape[-1]
    peers = lax.axis_size("tm")
    whole_rows = (
        frames == 1
        and lax.axis_size("band") == 2
        and lax.axis_size("parts") == 2
        and peers > 2
        and peers & (peers - 1) == 0
        and out_weight.shape[-1] % depth == 0
        and depth % (2 * HD) == 0
        and round_up(depth, 2 * LANES) > depth
    )
    run = fast if whole_rows else general
    return run(query_tokens, key_tokens, value_tokens, norm_gain, out_weight)


def solution(mesh):
    in_specs = (
        P(("parts", "tm"), "band", None, None),
        P(("parts", "tm"), "band", None, None),
        P(("parts", "tm"), "band", None, None),
        P(),
        P("band", "tm", None),
    )
    out_specs = P(("parts", "tm"), "band", None, None)
    return jax.shard_map(body, mesh=mesh, in_specs=in_specs, out_specs=out_specs, check_vma=False)
```

```python
import functools

import jax
import jax.numpy as jnp
from jax import lax
from jax.experimental import pallas as pl
from jax.experimental.pallas import tpu as pltpu
from jax.sharding import PartitionSpec as P


HEADS = 70
HD = 32
LANES = 128

norm_epsilon = 1e-06
read_epsilon = 1e-06


def round_up(n, m):
    return -(-n // m) * m


def call(kernel, out, args, scratch=(), flops=0, smem=0, mib=16, far_out=False):
    whole = pl.BlockSpec(memory_space=pltpu.VMEM)
    scalar = pl.BlockSpec(memory_space=pltpu.SMEM)
    far = pl.BlockSpec(memory_space=pl.ANY)
    moved = sum(a.size * a.dtype.itemsize for a in jax.tree.leaves((args, out)))
    return pl.pallas_call(
        kernel,
        out_shape=out,
        in_specs=[scalar] * smem + [whole] * (len(args) - smem),
        out_specs=jax.tree.map(lambda _: far if far_out else whole, out),
        scratch_shapes=list(scratch),
        compiler_params=pltpu.CompilerParams(vmem_limit_bytes=mib * 1024 * 1024),
        cost_estimate=pl.CostEstimate(flops=flops, bytes_accessed=moved, transcendentals=0),
    )(*args)


def line_ring(length):
    return [0, *range(1, length, 2), *reversed(range(2, length, 2))]


def ring_place(z, length):
    return jnp.where(z % 2 == 1, (z + 1) // 2, jnp.where(z == 0, 0, length - z // 2))


def at_ring_place(p, length):
    return jnp.where(p == 0, 0, jnp.where(p <= length // 2, 2 * p - 1, 2 * (length - p)))


def shape(dims, dtype):
    return jax.ShapeDtypeStruct(tuple(dims), dtype)


def unpack_weight(rows, depth, at_ref, w_ref, mine_ref, rest_ref, tall):
    half = mine_ref.shape[1]
    tall[pl.ds(rows // 8 * 8, tall.shape[0] - rows // 8 * 8), :] = jnp.zeros(
        (tall.shape[0] - rows // 8 * 8, tall.shape[1]), jnp.float32
    )
    edge = depth // LANES * LANES
    tall[:, pl.ds(edge, tall.shape[1] - edge)] = jnp.zeros(
        (tall.shape[0], tall.shape[1] - edge), jnp.float32
    )
    for r in range(rows):
        tall[r : r + 1, 0:depth] = w_ref[0, :, depth * r : depth * (r + 1)].astype(jnp.float32)
    y = at_ref[0]
    for ref, side in ((mine_ref, y), (rest_ref, 1 - y)):
        ref[...] = tall[:, pl.ds(pl.multiple_of(side * half, LANES), half)].astype(jnp.bfloat16)


def head_mask():
    row = lax.broadcasted_iota(jnp.int32, (LANES, LANES), 0) // HD
    lane = lax.broadcasted_iota(jnp.int32, (LANES, LANES), 1) // HD
    return row == lane


def state_sums(half, at_ref, k_ref, v_ref, own_ref, other_ref, sums):
    depth = k_ref.shape[1]
    mask = head_mask()
    sums[...] = jnp.zeros_like(sums)
    for start in range(0, depth, LANES):
        n = min(LANES, depth - start)
        keys = jnp.maximum(k_ref[:, start : start + n], 0)
        values = v_ref[:, start : start + n]
        outer = lax.dot_general(
            values, keys, (((0,), (0,)), ((), ())), preferred_element_type=jnp.float32
        )
        outer = jnp.where(mask[:n, :n], outer, 0.0)
        folded = sum(outer[i : i + HD] for i in range(0, n, HD))
        sums[0:HD, start : start + n] = folded
        sums[HD : HD + 1, start : start + n] = jnp.sum(
            keys.astype(jnp.float32), axis=0, keepdims=True
        )
    own_ref[...] = jnp.zeros_like(own_ref)
    other_ref[...] = jnp.zeros_like(other_ref)

    @pl.when(at_ref[1] == 0)
    def _():
        own_ref[:, 0:half] = sums[:, 0:half]
        other_ref[:, 0:half] = sums[:, half : 2 * half]

    @pl.when(at_ref[1] != 0)
    def _():
        own_ref[:, 0:half] = sums[:, half : 2 * half]
        other_ref[:, 0:half] = sums[:, 0:half]


def read_states(half, shard, slots, at_ref, q_ref, p_ref, g_ref, total_ref, *refs):
    steps = slots.bit_length() - 1
    scanned = refs[:steps]
    left_ref, square_ref, qh, gh, flat, blocks, s_ref = refs[steps:]
    s_ref[...] = total_ref[...]
    for step, got in enumerate(scanned):
        reached = (at_ref[2] >> step) % 2 == 1
        s_ref[...] += jnp.where(reached, got[...].astype(jnp.float32), 0.0)
    count = q_ref.shape[0]
    qh[...] = jnp.zeros_like(qh)
    gh[...] = jnp.zeros_like(gh)

    def take(first):
        qh[0:count, 0:half] = q_ref[:, first : first + half]
        qh[count : 2 * count, 0:half] = p_ref[:, first : first + half]
        gh[:, 0:half] = g_ref[:, first : first + half]

    @pl.when(at_ref[1] == 0)
    def _():
        take(0)

    @pl.when(at_ref[1] != 0)
    def _():
        take(half)

    mask = head_mask()
    square = jnp.zeros((2 * count, LANES), jnp.float32)
    for start in range(0, qh.shape[1], LANES):
        query = jnp.maximum(qh[:, start : start + LANES], 0)
        state = s_ref[0:HD, start : start + LANES]
        total = s_ref[HD : HD + 1, start : start + LANES]
        spread = jnp.concatenate(
            [
                jnp.where(mask, jnp.concatenate([state] * (LANES // HD), axis=0), 0.0),
                jnp.where(mask, jnp.broadcast_to(total, (LANES, LANES)), 0.0),
            ],
            axis=0,
        )
        high = spread.astype(jnp.bfloat16)
        low = (spread - high.astype(jnp.float32)).astype(jnp.bfloat16)
        both = lax.dot_general(
            jnp.concatenate([query, query], axis=1),
            jnp.concatenate([high, low], axis=1),
            (((1,), (1,)), ((), ())),
            preferred_element_type=jnp.float32,
        )
        reads = both[:, 0:LANES] / (both[:, LANES : 2 * LANES] + read_epsilon)
        square += reads * reads
        flat[:, start : start + LANES] = (reads * gh[:, start : start + LANES]).astype(jnp.bfloat16)
    square_ref[...] = jnp.broadcast_to(
        jnp.sum(square, axis=1, keepdims=True), square_ref.shape
    )
    wide = left_ref.shape[1] // slots
    blocks[...] = jnp.zeros_like(blocks)
    for t in range(slots):
        blocks[t, :, 0:shard] = flat[:, shard * t : shard * (t + 1)]
    length = slots // 2
    z, x = at_ref[2] // 2, at_ref[2] % 2
    place = ring_place(z, length)
    for m in range(slots):
        source = at_ring_place((place + length - m // 2) % length, length)
        left_ref[:, wide * m : wide * (m + 1)] = blocks[2 * source + (x ^ (m % 2))]


def product(left_ref, first, last, slots, pieces):
    weight = jnp.concatenate(
        [ref[...] if part is None else ref[part] for ref, part in pieces], axis=0
    )
    wide = weight.shape[0] // len(slots)
    left = jnp.concatenate(
        [left_ref[first:last, wide * m : wide * (m + 1)] for m in slots], axis=1
    )
    return jnp.dot(left, weight, preferred_element_type=jnp.float32)


def project_early(sides, plan, left_ref, *refs):
    outs = refs[-4:]
    count = outs[0].shape[0]
    for i, slots in enumerate(sides):
        pieces = [(refs[place], part) for place, part in plan[i]]
        total = product(left_ref, 0, 2 * count, slots, pieces)
        outs[2 * i][...] = total[:count]
        outs[2 * i + 1][...] = total[count:]


def project_late(first, last, slots, left_ref, base_ref, *refs):
    out_ref = refs[-1]
    pieces = [(ref, None) for ref in refs[:-1]]
    total = base_ref[...] + product(left_ref, first, last, slots, pieces)
    out_ref[...] = total.astype(out_ref.dtype)


def scaled(depth, square_ref, near_ref, own_ref, got_ref, out_ref):
    square = square_ref[0 : own_ref.shape[0], 0:1] + near_ref[:, 0:1]
    total = own_ref[...] + got_ref[...].astype(jnp.float32)
    out_ref[...] = (total * lax.rsqrt(square / depth + norm_epsilon)).astype(jnp.bfloat16)


def finish(
    depth, at_ref, square_ref, near_ref, mine_ref, got_mine_ref, rest_ref, out_ref, wide, sems
):
    count, half = mine_ref.shape
    each = count // sems.shape[0]

    def store(i):
        rows = pl.ds(i * each, each)
        return pltpu.make_async_copy(wide.at[rows], out_ref.at[rows], sems.at[i])

    def fill(mine_first):
        for i in range(sems.shape[0]):
            rows = slice(i * each, (i + 1) * each)
            square = square_ref[rows, 0:1] + near_ref[rows, 0:1]
            total = mine_ref[rows, :] + got_mine_ref[rows, :].astype(jnp.float32)
            mine = (total * lax.rsqrt(square / depth + norm_epsilon)).astype(jnp.bfloat16)
            rest = rest_ref[rows, :]
            left, right = (mine, rest) if mine_first else (rest, mine)
            wide[rows, 0:half] = left
            wide[rows, half:depth] = right[:, : depth - half]
            store(i).start()

    @pl.when(at_ref[0] == 0)
    def _():
        fill(True)

    @pl.when(at_ref[0] != 0)
    def _():
        fill(False)

    for i in range(sems.shape[0]):
        store(i).wait()


def fast(query_tokens, key_tokens, value_tokens, norm_gain, out_weight):
    frames, rows, width, depth = query_tokens.shape
    count = rows * width
    bands, peers = lax.axis_size("band"), lax.axis_size("tm")
    half = depth // bands
    wide = round_up(half, LANES)
    shard = out_weight.shape[-1] // depth
    tall = round_up(shard, 16)
    cols = round_up(depth, 2 * LANES) // 2
    swap = [(0, 1), (1, 0)]

    def flip(x, mask):
        return lax.ppermute(x, "tm", [(i, i ^ mask) for i in range(peers)])

    def across(x, axis):
        return lax.ppermute(x, axis, swap)

    at = jnp.stack(
        [lax.axis_index("parts"), lax.axis_index("band"), lax.axis_index("tm")]
    ).astype(jnp.int32)
    bf16, f32 = jnp.bfloat16, jnp.float32

    mine, rest = {}, {}
    mine[0], rest[0] = call(
        functools.partial(unpack_weight, shard, depth),
        (shape((tall, cols), bf16), shape((tall, cols), bf16)),
        (at, out_weight),
        scratch=[pltpu.VMEM((tall, 2 * cols), f32)],
        smem=1,
    )
    length = peers // 2
    order = line_ring(length)
    onward = [
        (2 * a + x, 2 * b + x) for a, b in zip(order, order[1:] + order[:1]) for x in range(2)
    ]
    mine[1], rest[1] = flip(mine[0], 1), flip(rest[0], 1)
    for k in range(1, length):
        m = 2 * k
        mine[m] = lax.ppermute(mine[m - 2], "tm", onward)
        rest[m] = across(mine[m], "parts")
        if k < length - 1:
            mine[m + 1] = lax.ppermute(mine[m - 1], "tm", onward)
        else:
            mine[m + 1] = flip(mine[m], 1)
        if k == length - 1:
            rest[m + 1] = across(mine[m + 1], "parts")
        else:
            rest[m + 1] = flip(rest[m], 1)

    queries = query_tokens.reshape(count, depth)
    partner = across(query_tokens, "band").reshape(count, depth)
    own, other = call(
        functools.partial(state_sums, half),
        (shape((HD + 8, wide), f32), shape((HD + 8, wide), f32)),
        (at, key_tokens.reshape(count, depth), value_tokens.reshape(count, depth)),
        scratch=[pltpu.VMEM((HD + 8, round_up(depth, LANES)), f32)],
        smem=1,
        flops=2 * count * LANES * depth,
    )
    total = own + across(other, "band")
    sent = total.astype(bf16)
    running, scanned = total, []
    while 1 << len(scanned) < peers:
        step = len(scanned)
        scanned.append(flip(sent, 1 << step))
        running = running + scanned[-1].astype(f32)
        sent = running.astype(bf16)
    left, square = call(
        functools.partial(read_states, half, shard, peers),
        (shape((2 * count, peers * tall), bf16), shape((2 * count, LANES), f32)),
        (at, queries, partner, norm_gain.reshape(1, depth), total, *scanned),
        scratch=[
            pltpu.VMEM((2 * count, wide), bf16),
            pltpu.VMEM((1, wide), f32),
            pltpu.VMEM((2 * count, wide), bf16),
            pltpu.VMEM((peers, 2 * count, tall), bf16),
            pltpu.VMEM((HD + 8, wide), f32),
        ],
        smem=1,
        flops=8 * count * LANES * wide,
    )

    near_square = across(square[count:], "band")
    late = ((peers - 3,), (peers - 3, peers - 1))
    soon = tuple(tuple(m for m in range(peers) if m not in side) for side in late)
    arrays, plan = [], []
    for chosen, held in zip(soon, (mine, rest)):
        plan.append([])
        for m in chosen:
            array, part = held[m] if isinstance(held[m], tuple) else (held[m], None)
            if not any(array is a for a in arrays):
                arrays.append(array)
            plan[-1].append(([array is a for a in arrays].index(True), part))
    base = call(
        functools.partial(project_early, soon, plan),
        (shape((count, cols), f32),) * 4,
        (left, *arrays),
        flops=4 * count * cols * tall * sum(map(len, plan)),
    )

    def finished(side, held):
        first = 2 * side
        sums = []
        for which, rows_from, dtype in (("other", count, bf16), ("own", 0, f32)):
            sums.append(
                call(
                    functools.partial(project_late, rows_from, rows_from + count, late[side]),
                    shape((count, cols), dtype),
                    (left, base[first + (which == "other")], *[held[m] for m in late[side]]),
                    flops=2 * count * cols * tall * len(late[side]),
                )
            )
        return sums[1], across(sums[0], "band")

    from_rest = finished(1, rest)
    from_mine = finished(0, mine)
    rest_out = call(
        functools.partial(scaled, depth),
        shape((count, cols), bf16),
        (square, near_square, *from_rest),
    )
    out = call(
        functools.partial(finish, depth),
        shape((count, depth), bf16),
        (at, square, near_square, *from_mine, rest_out),
        scratch=[pltpu.VMEM((count, depth), bf16), pltpu.SemaphoreType.DMA((4,))],
        smem=1,
        far_out=True,
    )
    return out.reshape(frames, rows, width, depth)


def entering(x, axis, combine, identity):
    peers, place = (lax.axis_size(axis), lax.axis_index(axis))
    everything = jax.tree.map(lambda part: lax.all_gather(part, axis), x)
    start = jax.tree.map(
        lambda part, zero: jnp.broadcast_to(jnp.asarray(zero, part.dtype), part.shape), x, identity
    )

    def hop(k, before):
        reached = k < place
        new = combine(before, jax.tree.map(lambda part: part[k], everything))
        return jax.tree.map(lambda a, b: jnp.where(reached, a, b), new, before)

    return lax.fori_loop(0, peers, hop, start)


def add_pair(earlier, later):
    return (earlier[0] + later[0], earlier[1] + later[1])


def general(query_tokens, key_tokens, value_tokens, norm_gain, out_weight):
    frames, rows, width, depth = query_tokens.shape
    key_relu = jax.nn.relu(key_tokens).reshape(frames, rows * width, HEADS, HD)
    value_heads = value_tokens.reshape(frames, rows * width, HEADS, HD)
    part_state = jnp.einsum(
        "fthd,fthe->fhde", key_relu, value_heads, preferred_element_type=jnp.float32
    ).reshape(frames, HEADS, HD * HD)
    part_norm = jnp.sum(key_relu, axis=1, dtype=jnp.float32)
    state_sum, norm_sum = lax.psum((part_state, part_norm), "band")
    local_state = jnp.cumsum(state_sum, axis=0)
    local_norm = jnp.cumsum(norm_sum, axis=0)
    before = entering(
        (local_state[-1], local_norm[-1]),
        "tm",
        add_pair,
        (jnp.zeros_like(local_state[-1]), jnp.zeros_like(local_norm[-1])),
    )
    prefix_state = local_state + before[0]
    prefix_norm = local_norm + before[1]
    query_relu = jax.nn.relu(query_tokens.astype(jnp.float32)).reshape(
        frames, rows * width, HEADS, HD
    )
    numer = jnp.einsum(
        "fthd,fhde->fthe",
        query_relu,
        prefix_state.reshape(frames, HEADS, HD, HD),
        precision=lax.Precision.HIGHEST,
    )
    denom = (
        jnp.einsum("fthd,fhd->fth", query_relu, prefix_norm, precision=lax.Precision.HIGHEST)
        + read_epsilon
    )
    reads = (numer / denom[:, :, :, None]).reshape(frames * rows * width, depth)
    square = jnp.mean(reads * reads, axis=-1, keepdims=True)
    normed = (reads * lax.rsqrt(square + norm_epsilon) * norm_gain).astype(jnp.bfloat16)
    gathered = lax.all_gather(out_weight, "tm", axis=1, tiled=True)
    rows_half = gathered.reshape(-1, depth)
    result = jnp.dot(
        normed,
        lax.all_gather(rows_half, "band", axis=0, tiled=True),
        preferred_element_type=jnp.float32,
    )
    return result.astype(jnp.bfloat16).reshape(frames, rows, width, depth)


def body(query_tokens, key_tokens, value_tokens, norm_gain, out_weight):
    frames, depth = query_tokens.shape[0], query_tokens.shape[-1]
    peers = lax.axis_size("tm")
    whole_rows = (
        frames == 1
        and lax.axis_size("band") == 2
        and lax.axis_size("parts") == 2
        and peers > 2
        and query_tokens.shape[1] * query_tokens.shape[2] % 64 == 0
        and peers & (peers - 1) == 0
        and out_weight.shape[-1] % depth == 0
        and depth % (2 * HD) == 0
        and round_up(depth, 2 * LANES) > depth
    )
    run = fast if whole_rows else general
    return run(query_tokens, key_tokens, value_tokens, norm_gain, out_weight)


def solution(mesh):
    in_specs = (
        P(("parts", "tm"), "band", None, None),
        P(("parts", "tm"), "band", None, None),
        P(("parts", "tm"), "band", None, None),
        P(),
        P("band", "tm", None),
    )
    out_specs = P(("parts", "tm"), "band", None, None)
    return jax.shard_map(body, mesh=mesh, in_specs=in_specs, out_specs=out_specs, check_vma=False)
```

```python
import functools

import jax
import jax.numpy as jnp
from jax import lax
from jax.experimental import pallas as pl
from jax.experimental.pallas import tpu as pltpu
from jax.sharding import PartitionSpec as P


HEADS = 70
HD = 32
LANES = 128

norm_epsilon = 1e-06
read_epsilon = 1e-06


def round_up(n, m):
    return -(-n // m) * m


def call(kernel, out, args, scratch=(), flops=0, smem=0, mib=16):
    whole = pl.BlockSpec(memory_space=pltpu.VMEM)
    scalar = pl.BlockSpec(memory_space=pltpu.SMEM)
    moved = sum(a.size * a.dtype.itemsize for a in jax.tree.leaves((args, out)))
    return pl.pallas_call(
        kernel,
        out_shape=out,
        in_specs=[scalar] * smem + [whole] * (len(args) - smem),
        out_specs=jax.tree.map(lambda _: whole, out),
        scratch_shapes=list(scratch),
        compiler_params=pltpu.CompilerParams(vmem_limit_bytes=mib * 1024 * 1024),
        cost_estimate=pl.CostEstimate(flops=flops, bytes_accessed=moved, transcendentals=0),
    )(*args)


def line_ring(length):
    return [0, *range(1, length, 2), *reversed(range(2, length, 2))]


def ring_place(z, length):
    return jnp.where(z % 2 == 1, (z + 1) // 2, jnp.where(z == 0, 0, length - z // 2))


def at_ring_place(p, length):
    return jnp.where(p == 0, 0, jnp.where(p <= length // 2, 2 * p - 1, 2 * (length - p)))


def shape(dims, dtype):
    return jax.ShapeDtypeStruct(tuple(dims), dtype)


def unpack_weight(rows, depth, at_ref, w_ref, mine_ref, rest_ref, tall):
    half = mine_ref.shape[1]
    tall[pl.ds(rows // 8 * 8, tall.shape[0] - rows // 8 * 8), :] = jnp.zeros(
        (tall.shape[0] - rows // 8 * 8, tall.shape[1]), jnp.float32
    )
    edge = depth // LANES * LANES
    tall[:, pl.ds(edge, tall.shape[1] - edge)] = jnp.zeros(
        (tall.shape[0], tall.shape[1] - edge), jnp.float32
    )
    for r in range(rows):
        tall[r : r + 1, 0:depth] = w_ref[0, :, depth * r : depth * (r + 1)].astype(jnp.float32)
    y = at_ref[0]
    for ref, side in ((mine_ref, y), (rest_ref, 1 - y)):
        ref[...] = tall[:, pl.ds(pl.multiple_of(side * half, LANES), half)].astype(jnp.bfloat16)


def head_mask():
    row = lax.broadcasted_iota(jnp.int32, (LANES, LANES), 0) // HD
    lane = lax.broadcasted_iota(jnp.int32, (LANES, LANES), 1) // HD
    return row == lane


def state_sums(half, at_ref, k_ref, v_ref, own_ref, other_ref, sums):
    depth = k_ref.shape[1]
    mask = head_mask()
    sums[...] = jnp.zeros_like(sums)
    for start in range(0, depth, LANES):
        n = min(LANES, depth - start)
        keys = jnp.maximum(k_ref[:, start : start + n], 0)
        values = v_ref[:, start : start + n]
        outer = lax.dot_general(
            values, keys, (((0,), (0,)), ((), ())), preferred_element_type=jnp.float32
        )
        outer = jnp.where(mask[:n, :n], outer, 0.0)
        folded = sum(outer[i : i + HD] for i in range(0, n, HD))
        sums[0:HD, start : start + n] = folded
        sums[HD : HD + 1, start : start + n] = jnp.sum(
            keys.astype(jnp.float32), axis=0, keepdims=True
        )
    own_ref[...] = jnp.zeros_like(own_ref)
    other_ref[...] = jnp.zeros_like(other_ref)

    @pl.when(at_ref[1] == 0)
    def _():
        own_ref[:, 0:half] = sums[:, 0:half]
        other_ref[:, 0:half] = sums[:, half : 2 * half]

    @pl.when(at_ref[1] != 0)
    def _():
        own_ref[:, 0:half] = sums[:, half : 2 * half]
        other_ref[:, 0:half] = sums[:, 0:half]


def read_states(half, shard, slots, at_ref, q_ref, p_ref, g_ref, total_ref, *refs):
    steps = slots.bit_length() - 1
    scanned = refs[:steps]
    left_ref, square_ref, qh, gh, flat, blocks, s_ref = refs[steps:]
    s_ref[...] = total_ref[...]
    for step, got in enumerate(scanned):
        reached = (at_ref[2] >> step) % 2 == 1
        s_ref[...] += jnp.where(reached, got[...].astype(jnp.float32), 0.0)
    count = q_ref.shape[0]
    qh[...] = jnp.zeros_like(qh)
    gh[...] = jnp.zeros_like(gh)

    def take(first):
        qh[0:count, 0:half] = q_ref[:, first : first + half]
        qh[count : 2 * count, 0:half] = p_ref[:, first : first + half]
        gh[:, 0:half] = g_ref[:, first : first + half]

    @pl.when(at_ref[1] == 0)
    def _():
        take(0)

    @pl.when(at_ref[1] != 0)
    def _():
        take(half)

    mask = head_mask()
    square = jnp.zeros((2 * count, LANES), jnp.float32)
    for start in range(0, qh.shape[1], LANES):
        query = jnp.maximum(qh[:, start : start + LANES], 0)
        state = s_ref[0:HD, start : start + LANES]
        total = s_ref[HD : HD + 1, start : start + LANES]
        spread = jnp.concatenate(
            [
                jnp.where(mask, jnp.concatenate([state] * (LANES // HD), axis=0), 0.0),
                jnp.where(mask, jnp.broadcast_to(total, (LANES, LANES)), 0.0),
            ],
            axis=0,
        )
        high = spread.astype(jnp.bfloat16)
        low = (spread - high.astype(jnp.float32)).astype(jnp.bfloat16)
        both = lax.dot_general(
            jnp.concatenate([query, query], axis=1),
            jnp.concatenate([high, low], axis=1),
            (((1,), (1,)), ((), ())),
            preferred_element_type=jnp.float32,
        )
        reads = both[:, 0:LANES] / (both[:, LANES : 2 * LANES] + read_epsilon)
        square += reads * reads
        flat[:, start : start + LANES] = (reads * gh[:, start : start + LANES]).astype(jnp.bfloat16)
    square_ref[...] = jnp.broadcast_to(
        jnp.sum(square, axis=1, keepdims=True), square_ref.shape
    )
    wide = left_ref.shape[1] // slots
    blocks[...] = jnp.zeros_like(blocks)
    for t in range(slots):
        blocks[t, :, 0:shard] = flat[:, shard * t : shard * (t + 1)]
    length = slots // 2
    z, x = at_ref[2] // 2, at_ref[2] % 2
    place = ring_place(z, length)
    for m in range(slots):
        source = at_ring_place((place + length - m // 2) % length, length)
        left_ref[:, wide * m : wide * (m + 1)] = blocks[2 * source + (x ^ (m % 2))]


def product(left_ref, first, last, slots, pieces):
    weight = jnp.concatenate(
        [ref[...] if part is None else ref[part] for ref, part in pieces], axis=0
    )
    wide = weight.shape[0] // len(slots)
    left = jnp.concatenate(
        [left_ref[first:last, wide * m : wide * (m + 1)] for m in slots], axis=1
    )
    return jnp.dot(left, weight, preferred_element_type=jnp.float32)


def project_early(sides, plan, left_ref, *refs):
    outs = refs[-4:]
    count = outs[0].shape[0]
    for i, slots in enumerate(sides):
        pieces = [(refs[place], part) for place, part in plan[i]]
        total = product(left_ref, 0, 2 * count, slots, pieces)
        outs[2 * i][...] = total[:count]
        outs[2 * i + 1][...] = total[count:]


def project_late(first, last, slots, left_ref, base_ref, *refs):
    out_ref = refs[-1]
    pieces = [(ref, None) for ref in refs[:-1]]
    total = base_ref[...] + product(left_ref, first, last, slots, pieces)
    out_ref[...] = total.astype(out_ref.dtype)


def scaled(depth, square_ref, near_ref, own_ref, got_ref, out_ref):
    square = square_ref[0 : own_ref.shape[0], 0:1] + near_ref[:, 0:1]
    total = own_ref[...] + got_ref[...].astype(jnp.float32)
    out_ref[...] = (total * lax.rsqrt(square / depth + norm_epsilon)).astype(jnp.bfloat16)


def finish(depth, at_ref, square_ref, near_ref, mine_ref, got_mine_ref, rest_ref, out_ref):
    count, half = mine_ref.shape
    square = square_ref[0:count, 0:1] + near_ref[:, 0:1]
    total = mine_ref[...] + got_mine_ref[...].astype(jnp.float32)
    mine = (total * lax.rsqrt(square / depth + norm_epsilon)).astype(jnp.bfloat16)

    @pl.when(at_ref[0] == 0)
    def _():
        out_ref[:, 0:half] = mine
        out_ref[:, half:depth] = rest_ref[:, : depth - half]

    @pl.when(at_ref[0] != 0)
    def _():
        out_ref[:, 0:half] = rest_ref[...]
        out_ref[:, half:depth] = mine[:, : depth - half]


def fast(query_tokens, key_tokens, value_tokens, norm_gain, out_weight):
    frames, rows, width, depth = query_tokens.shape
    count = rows * width
    bands, peers = lax.axis_size("band"), lax.axis_size("tm")
    half = depth // bands
    wide = round_up(half, LANES)
    shard = out_weight.shape[-1] // depth
    tall = round_up(shard, 16)
    cols = round_up(depth, 2 * LANES) // 2
    swap = [(0, 1), (1, 0)]

    def flip(x, mask):
        return lax.ppermute(x, "tm", [(i, i ^ mask) for i in range(peers)])

    def across(x, axis):
        return lax.ppermute(x, axis, swap)

    at = jnp.stack(
        [lax.axis_index("parts"), lax.axis_index("band"), lax.axis_index("tm")]
    ).astype(jnp.int32)
    bf16, f32 = jnp.bfloat16, jnp.float32

    mine, rest = {}, {}
    mine[0], rest[0] = call(
        functools.partial(unpack_weight, shard, depth),
        (shape((tall, cols), bf16), shape((tall, cols), bf16)),
        (at, out_weight),
        scratch=[pltpu.VMEM((tall, 2 * cols), f32)],
        smem=1,
    )
    length = peers // 2
    order = line_ring(length)
    onward = [
        (2 * a + x, 2 * b + x) for a, b in zip(order, order[1:] + order[:1]) for x in range(2)
    ]
    mine[1], rest[1] = flip(mine[0], 1), flip(rest[0], 1)
    for k in range(1, length):
        m = 2 * k
        mine[m] = lax.ppermute(mine[m - 2], "tm", onward)
        rest[m] = across(mine[m], "parts")
        if k < length - 1:
            mine[m + 1] = lax.ppermute(mine[m - 1], "tm", onward)
        else:
            mine[m + 1] = flip(mine[m], 1)
        if k == length - 1:
            rest[m + 1] = across(mine[m + 1], "parts")
        else:
            rest[m + 1] = flip(rest[m], 1)

    queries = query_tokens.reshape(count, depth)
    partner = across(query_tokens, "band").reshape(count, depth)
    own, other = call(
        functools.partial(state_sums, half),
        (shape((HD + 8, wide), f32), shape((HD + 8, wide), f32)),
        (at, key_tokens.reshape(count, depth), value_tokens.reshape(count, depth)),
        scratch=[pltpu.VMEM((HD + 8, round_up(depth, LANES)), f32)],
        smem=1,
        flops=2 * count * LANES * depth,
    )
    total = own + across(other, "band")
    sent = total.astype(bf16)
    running, scanned = total, []
    while 1 << len(scanned) < peers:
        step = len(scanned)
        scanned.append(flip(sent, 1 << step))
        running = running + scanned[-1].astype(f32)
        sent = running.astype(bf16)
    left, square = call(
        functools.partial(read_states, half, shard, peers),
        (shape((2 * count, peers * tall), bf16), shape((2 * count, LANES), f32)),
        (at, queries, partner, norm_gain.reshape(1, depth), total, *scanned),
        scratch=[
            pltpu.VMEM((2 * count, wide), bf16),
            pltpu.VMEM((1, wide), f32),
            pltpu.VMEM((2 * count, wide), bf16),
            pltpu.VMEM((peers, 2 * count, tall), bf16),
            pltpu.VMEM((HD + 8, wide), f32),
        ],
        smem=1,
        flops=8 * count * LANES * wide,
    )

    near_square = across(square[count:], "band")
    late = ((peers - 3,), (peers - 3, peers - 1))
    soon = tuple(tuple(m for m in range(peers) if m not in side) for side in late)
    arrays, plan = [], []
    for chosen, held in zip(soon, (mine, rest)):
        plan.append([])
        for m in chosen:
            array, part = held[m] if isinstance(held[m], tuple) else (held[m], None)
            if not any(array is a for a in arrays):
                arrays.append(array)
            plan[-1].append(([array is a for a in arrays].index(True), part))
    base = call(
        functools.partial(project_early, soon, plan),
        (shape((count, cols), f32),) * 4,
        (left, *arrays),
        flops=4 * count * cols * tall * sum(map(len, plan)),
    )

    def finished(side, held):
        first = 2 * side
        sums = []
        for which, rows_from, dtype in (("other", count, bf16), ("own", 0, f32)):
            sums.append(
                call(
                    functools.partial(project_late, rows_from, rows_from + count, late[side]),
                    shape((count, cols), dtype),
                    (left, base[first + (which == "other")], *[held[m] for m in late[side]]),
                    flops=2 * count * cols * tall * len(late[side]),
                )
            )
        return sums[1], across(sums[0], "band")

    from_rest = finished(1, rest)
    from_mine = finished(0, mine)
    rest_out = call(
        functools.partial(scaled, depth),
        shape((count, cols), bf16),
        (square, near_square, *from_rest),
    )
    out = call(
        functools.partial(finish, depth),
        shape((count, depth), bf16),
        (at, square, near_square, *from_mine, rest_out),
        smem=1,
    )
    return out.reshape(frames, rows, width, depth)


def entering(x, axis, combine, identity):
    peers, place = (lax.axis_size(axis), lax.axis_index(axis))
    everything = jax.tree.map(lambda part: lax.all_gather(part, axis), x)
    start = jax.tree.map(
        lambda part, zero: jnp.broadcast_to(jnp.asarray(zero, part.dtype), part.shape), x, identity
    )

    def hop(k, before):
        reached = k < place
        new = combine(before, jax.tree.map(lambda part: part[k], everything))
        return jax.tree.map(lambda a, b: jnp.where(reached, a, b), new, before)

    return lax.fori_loop(0, peers, hop, start)


def add_pair(earlier, later):
    return (earlier[0] + later[0], earlier[1] + later[1])


def general(query_tokens, key_tokens, value_tokens, norm_gain, out_weight):
    frames, rows, width, depth = query_tokens.shape
    key_relu = jax.nn.relu(key_tokens).reshape(frames, rows * width, HEADS, HD)
    value_heads = value_tokens.reshape(frames, rows * width, HEADS, HD)
    part_state = jnp.einsum(
        "fthd,fthe->fhde", key_relu, value_heads, preferred_element_type=jnp.float32
    ).reshape(frames, HEADS, HD * HD)
    part_norm = jnp.sum(key_relu, axis=1, dtype=jnp.float32)
    state_sum, norm_sum = lax.psum((part_state, part_norm), "band")
    local_state = jnp.cumsum(state_sum, axis=0)
    local_norm = jnp.cumsum(norm_sum, axis=0)
    before = entering(
        (local_state[-1], local_norm[-1]),
        "tm",
        add_pair,
        (jnp.zeros_like(local_state[-1]), jnp.zeros_like(local_norm[-1])),
    )
    prefix_state = local_state + before[0]
    prefix_norm = local_norm + before[1]
    query_relu = jax.nn.relu(query_tokens.astype(jnp.float32)).reshape(
        frames, rows * width, HEADS, HD
    )
    numer = jnp.einsum(
        "fthd,fhde->fthe",
        query_relu,
        prefix_state.reshape(frames, HEADS, HD, HD),
        precision=lax.Precision.HIGHEST,
    )
    denom = (
        jnp.einsum("fthd,fhd->fth", query_relu, prefix_norm, precision=lax.Precision.HIGHEST)
        + read_epsilon
    )
    reads = (numer / denom[:, :, :, None]).reshape(frames * rows * width, depth)
    square = jnp.mean(reads * reads, axis=-1, keepdims=True)
    normed = (reads * lax.rsqrt(square + norm_epsilon) * norm_gain).astype(jnp.bfloat16)
    gathered = lax.all_gather(out_weight, "tm", axis=1, tiled=True)
    rows_half = gathered.reshape(-1, depth)
    result = jnp.dot(
        normed,
        lax.all_gather(rows_half, "band", axis=0, tiled=True),
        preferred_element_type=jnp.float32,
    )
    return result.astype(jnp.bfloat16).reshape(frames, rows, width, depth)


def body(query_tokens, key_tokens, value_tokens, norm_gain, out_weight):
    frames, depth = query_tokens.shape[0], query_tokens.shape[-1]
    peers = lax.axis_size("tm")
    whole_rows = (
        frames == 1
        and lax.axis_size("band") == 2
        and lax.axis_size("parts") == 2
        and peers > 2
        and peers & (peers - 1) == 0
        and out_weight.shape[-1] % depth == 0
        and depth % (2 * HD) == 0
        and round_up(depth, 2 * LANES) > depth
    )
    run = fast if whole_rows else general
    return run(query_tokens, key_tokens, value_tokens, norm_gain, out_weight)


def solution(mesh):
    in_specs = (
        P(("parts", "tm"), "band", None, None),
        P(("parts", "tm"), "band", None, None),
        P(("parts", "tm"), "band", None, None),
        P(),
        P("band", "tm", None),
    )
    out_specs = P(("parts", "tm"), "band", None, None)
    return jax.shard_map(body, mesh=mesh, in_specs=in_specs, out_specs=out_specs, check_vma=False)
```
